512 devices in a mesh: tile: 64 (over z, x, core), freq: 8 (over y).
Axes of the slice: x: 4, y: 8, z: 8, core: 2. Of those that a mesh axis runs over, the one named last changes fastest.
Arguments:
- u_factors: bfloat16 [8, 16384, 32, 128], P('freq', 'tile'), may hold values from -0.125 to 0.125
- v_factors: bfloat16 [8, 16384, 32, 128], P('freq', 'tile'), may hold values from -0.1875 to 0.1875
- ranks: int32 [8, 32, 32], P('freq'), may hold values from 8 to 64, as said below
- observed: float32 [8, 16384, 128], P('freq', 'tile'), may hold values from -6 to 6
- start: float32 [8, 16384, 128], P('freq', 'tile'), may hold values from -6 to 6
Outputs:
- estimate: float32 [8, 16384, 128], P('freq', 'tile')
The draws below stay inside these ranges and needn't reach their ends.
Inputs may be any that keep to these rules, and one draw needn't show every extreme that they name: `ranks`: every frequency has a tile of rank 64 and a tile of rank 64 // 8.
All inputs are finite; a program needn't handle non-finite values.
Results may differ from the reference program's by a relative error of at most 0.0031.
Values may be sent and summed in bfloat16 or wider, within the bound.
A program may use at most 64 MiB of HBM per device.

```python
import math
import jax
import jax.numpy as jnp
from jax import lax

NS = 64
TILE = 512
RMAX = 64
ROUNDS = 1
STEPS = 1
TR = 32
TC = 32
NCOL = 16384
NROW = 16384
FREQS = 8
N_TILE = 64


def draw_ranks(key, part):
    least = RMAX // 8
    values = jax.random.randint(key, (FREQS, TR, TC), least, RMAX - least + 1)
    values = values.at[:, 0, 0].set(RMAX)
    values = values.at[:, 0, 1].set(least)
    return values.astype(jnp.int32)


def level_of(stream_key, extent, shards, low, high):
    factor_of, own = 1.0, jax.random.fold_in(stream_key, 6)
    for axis_at, shards_of in shards:
        draws = jnp.exp(jax.random.uniform(jax.random.fold_in(own, axis_at), (shards_of,), jnp.float32, low / len(shards), high / len(shards)))
        factor_of = factor_of * jnp.repeat(draws, extent[axis_at] // shards_of).reshape([-1 if axis == axis_at else 1 for axis in range(len(extent))])
    return factor_of


def normal_values(stream_key, dims, width, most, split=(), kind=jnp.bfloat16):
    result = jax.random.normal(stream_key, dims, jnp.float32) * width
    if len(split) > 0:
        result = level_of(stream_key, dims, split, -0.22, 0.18) * result
    return jnp.clip(result, min=-most, max=most).astype(kind)


def setup_inputs(seed: int = 0) -> dict:
    key_of = jax.random.split(jax.random.key(seed), 6)
    return {
        "u_factors": normal_values(key_of[0], (FREQS, NROW, TC, 2 * RMAX), (TC * RMAX) ** -0.5, 0.125, ((0, 8), (1, 64))),
        "v_factors": normal_values(key_of[1], (FREQS, NCOL, TR, 2 * RMAX), (2 * TILE) ** -0.5, 0.1875, ((0, 8), (1, 64))),
        "ranks": draw_ranks(jax.random.fold_in(key_of[5], 71), 0),
        "observed": normal_values(key_of[3], (FREQS, NROW, 2 * NS), 1.0, 6.0, ((0, 8), (1, 64)), jnp.float32),
        "start": normal_values(key_of[4], (FREQS, NCOL, 2 * NS), 1.0, 6.0, ((0, 8), (1, 64)), jnp.float32),
    }


STEP_SIZE = 0.2
LEVEL = 0.5
TOP_PRECISION = lax.Precision.HIGHEST

def round_low(values):
    return lax.optimization_barrier(values.astype(jnp.bfloat16))

def conj_product(blocks, rank_half, source_half):
    real_part = blocks[..., :rank_half, :source_half] + blocks[..., rank_half:, source_half:]
    imaginary = blocks[..., :rank_half, source_half:] - blocks[..., rank_half:, :source_half]
    return jnp.concatenate([real_part, imaginary], axis=-1)

def complex_stack(coeffs, source_half):
    lower_rows = jnp.concatenate([-coeffs[..., source_half:], coeffs[..., :source_half]], axis=-1)
    return jnp.concatenate([coeffs, lower_rows], axis=-2)

def band_tables(band_ids, band_size):
    phases = 2.0 * jnp.pi * band_ids.astype(jnp.float32)[:, None] * jnp.arange(band_size, dtype=jnp.float32)[None, :] / band_size
    return (jnp.cos(phases), jnp.sin(phases))

def to_time(spectra, cosine_matrix, sine_matrix):
    source_half = spectra.shape[-1] // 2
    factor = 1.0 / math.sqrt(cosine_matrix.shape[1])
    input_real = spectra[..., :source_half]
    imaginary_input = spectra[..., source_half:]
    output_real = jnp.einsum('bg,biq->giq', cosine_matrix, input_real, precision=TOP_PRECISION) - jnp.einsum('bg,biq->giq', sine_matrix, imaginary_input, precision=TOP_PRECISION)
    imaginary_output = jnp.einsum('bg,biq->giq', sine_matrix, input_real, precision=TOP_PRECISION) + jnp.einsum('bg,biq->giq', cosine_matrix, imaginary_input, precision=TOP_PRECISION)
    return jnp.concatenate([output_real, imaginary_output], axis=-1) * factor

def to_freq(samples, cosine_matrix, sine_matrix):
    source_half = samples.shape[-1] // 2
    factor = 1.0 / math.sqrt(cosine_matrix.shape[1])
    input_real = samples[..., :source_half]
    imaginary_input = samples[..., source_half:]
    output_real = jnp.einsum('be,evi->bvi', cosine_matrix, input_real, precision=TOP_PRECISION) + jnp.einsum('be,evi->bvi', sine_matrix, imaginary_input, precision=TOP_PRECISION)
    imaginary_output = jnp.einsum('be,evi->bvi', cosine_matrix, imaginary_input, precision=TOP_PRECISION) - jnp.einsum('be,evi->bvi', sine_matrix, input_real, precision=TOP_PRECISION)
    return jnp.concatenate([output_real, imaginary_output], axis=-1) * factor

def thin_out(values):
    return values - jnp.clip(values, -LEVEL, LEVEL)

def descend(operands):
    left_factor, right_factor, rank_table, observed_rows, estimate = operands
    half_tile = TILE // 2
    group_size = N_TILE // TR
    row_span = TR * TILE // N_TILE
    mask_table = (jnp.arange(RMAX, dtype=jnp.int32)[None, None, :] < rank_table[:, :, None]).astype(jnp.float32)[..., None]
    mask_columns = jnp.swapaxes(mask_table, 0, 1)
    right_halves = right_factor.astype(jnp.float32).reshape(TC, 2, half_tile, TR, 2 * RMAX)
    right_tiles = right_factor.astype(jnp.float32).reshape(TC, TILE, TR, 2 * RMAX)
    left_tiles = left_factor.astype(jnp.float32).reshape(TR, TILE, TC, 2 * RMAX)
    left_groups = left_factor.astype(jnp.float32).reshape(TR, group_size, row_span, TC, 2 * RMAX)
    for turn_index in range(STEPS):
        low = round_low(estimate).astype(jnp.float32).reshape(TC, 2, half_tile, 2 * NS)
        blocks = jnp.einsum('jhcik,jhcs->jhiks', right_halves, low)
        partial_value = round_low(conj_product(blocks, RMAX, NS)).astype(jnp.float32)
        coeffs = round_low((partial_value[:, 0] + partial_value[:, 1]) * mask_columns)
        image_rows = jnp.einsum('itjk,jiks->its', left_tiles, complex_stack(coeffs, NS).astype(jnp.float32)).reshape(TR * TILE, 2 * NS)
        misfit = image_rows - observed_rows
        misfit_low = round_low(misfit).astype(jnp.float32).reshape(TR, group_size, row_span, 2 * NS)
        back_blocks = jnp.einsum('igrjk,igrs->igjks', left_groups, misfit_low)
        back_part = round_low(conj_product(back_blocks, RMAX, NS)).astype(jnp.float32)
        back_coeffs = round_low(lax.optimization_barrier(jnp.sum(back_part, axis=1)) * mask_table)
        gradient = jnp.einsum('jcik,ijks->jcs', right_tiles, complex_stack(back_coeffs, NS).astype(jnp.float32)).reshape(TC * TILE, 2 * NS)
        estimate = estimate - STEP_SIZE * gradient
    return estimate

def reference(u_factors, v_factors, ranks, observed, start):
    estimate = start
    cosine_matrix, sine_matrix = band_tables(jnp.arange(FREQS, dtype=jnp.int32), FREQS)
    for round_index in range(ROUNDS):
        estimate = lax.map(descend, (u_factors, v_factors, ranks, observed, estimate))
        thinned = thin_out(to_time(estimate, cosine_matrix, sine_matrix))
        estimate = to_freq(thinned, cosine_matrix, sine_matrix)
    return estimate
```

```python
import math

import jax
import jax.numpy as jnp
from jax import lax
from jax.experimental import pallas as pl
from jax.experimental.pallas import tpu as pltpu
from jax.sharding import PartitionSpec as P

STEP_SIZE = 0.2
LEVEL = 0.5
PLANE = (8, 4)
BANDS = 8
MESH = pl.DeviceIdType.MESH
BF16 = jnp.bfloat16
F32 = jnp.float32


def far_first(extent):
    order = sorted(range(extent), key=lambda d: (-min(d, extent - d), d))
    return order


def twiddle_pair(real, imag, cosine, sine):
    if abs(sine) < 1e-9:
        return (real, imag) if cosine > 0 else (-real, -imag)
    if abs(cosine) < 1e-9:
        return (-imag, real) if sine > 0 else (imag, -real)
    return real * cosine - imag * sine, real * sine + imag * cosine


def small_dft(reals, imags, sign):
    count = len(reals)
    if count == 1:
        return reals, imags
    even_re, even_im = small_dft(reals[0::2], imags[0::2], sign)
    odd_re, odd_im = small_dft(reals[1::2], imags[1::2], sign)
    out_re, out_im = [None] * count, [None] * count
    half = count // 2
    for k in range(half):
        angle = sign * 2.0 * math.pi * k / count
        tr, ti = twiddle_pair(odd_re[k], odd_im[k], math.cos(angle), math.sin(angle))
        out_re[k], out_im[k] = even_re[k] + tr, even_im[k] + ti
        out_re[k + half], out_im[k + half] = even_re[k] - tr, even_im[k] - ti
    return out_re, out_im


def thin_out(values):
    return values - jnp.clip(values, -LEVEL, LEVEL)


def kernel(
    ranks_ref, u_hbm, v_hbm, observed_hbm, start_hbm, out_ref,
    u_raw, v_raw, u_tiles, v_tiles, observed_rows, start_rows, start_t,
    pair_out, pair_own, pair_in, chip_out, chip_in, share_in,
    band_out, band_in, thin_out_buf, thin_in,
    load_sem, pair_send, pair_recv, chip_send, chip_recv, share_send, share_recv,
    band_send, band_recv,
):
    zc, xc = PLANE
    group = xc // 2
    bands = BANDS
    rows = u_raw.shape[0]
    lanes = u_raw.shape[2]
    rank_half = lanes // 2
    sources2 = start_t.shape[0]
    sources = sources2 // 2
    per_band = sources // bands

    place = lax.axis_index("tile")
    band = lax.axis_index("freq")
    chip = lax.div(place, 2)
    core = lax.rem(place, 2)
    other = 1 - core
    z = lax.div(chip, xc)
    x = lax.rem(chip, xc)
    order = far_first(zc)

    def shift_of(m, h, owner):
        return 2 * h + lax.rem(owner + order[m], 2)

    def chip_at(m, h, owner, forward):
        dz, dx = order[m], shift_of(m, h, owner)
        if forward:
            return lax.rem(z + dz, zc) * xc + lax.rem(x + dx, xc)
        return lax.rem(z + zc - dz, zc) * xc + lax.rem(x + xc - dx, xc)

    def is_self(m, h):
        return order[m] == 0 and h == 0

    def at_tile(index):
        return {"tile": index}

    barrier = pltpu.get_barrier_semaphore()

    def hail(device):
        pl.semaphore_signal(barrier, inc=1, device_id=device, device_id_type=MESH)

    for m in range(zc):
        for h in range(group):
            target = chip_at(m, h, core, True) * 2 + core
            if is_self(m, h):
                pl.when(core == 1)(lambda target=target: hail(at_tile(target)))
            else:
                hail(at_tile(target))
    hail(at_tile(chip * 2 + other))
    for k in range(1, bands):
        hail({"freq": lax.rem(band + k, bands)})

    loads = [
        pltpu.make_async_copy(start_hbm, start_rows, load_sem.at[0]),
        pltpu.make_async_copy(v_hbm, v_raw, load_sem.at[1]),
        pltpu.make_async_copy(observed_hbm, observed_rows, load_sem.at[2]),
        pltpu.make_async_copy(u_hbm, u_raw, load_sem.at[3]),
    ]
    for load in loads:
        load.start()

    def retile(raw, tiles):
        def step(b, carry):
            at = pl.multiple_of(b * 16, 16)
            tiles[:, pl.ds(at, 16), :] = jnp.swapaxes(raw[pl.ds(at, 16)], 0, 1)
            return carry
        lax.fori_loop(0, rows // 16, step, 0)

    lane_ids = lax.broadcasted_iota(jnp.int32, (sources, lanes), 1)
    upper = lane_ids < rank_half
    rank_ids = jnp.where(upper, lane_ids, lane_ids - rank_half)
    sign = jnp.where(upper, 1.0, -1.0).astype(F32)

    def swap_halves(values):
        return jnp.concatenate([values[:, rank_half:], values[:, :rank_half]], axis=1)

    def tile_group(tiles, m, owner, forward):
        return jnp.concatenate(
            [tiles[chip_at(m, h, owner, forward)] for h in range(group)], axis=1
        )

    def pair_copy(p, m):
        return pltpu.make_async_remote_copy(
            src_ref=pair_out.at[p, m], dst_ref=pair_in.at[p, m],
            send_sem=pair_send.at[p, m], recv_sem=pair_recv.at[p, m],
            device_id=at_tile(chip * 2 + other), device_id_type=MESH,
        )

    def chip_copy(p, m, h):
        return pltpu.make_async_remote_copy(
            src_ref=chip_out.at[p, m, h], dst_ref=chip_in.at[p, m, h],
            send_sem=chip_send.at[p, m, h], recv_sem=chip_recv.at[p, m, h],
            device_id=at_tile(chip_at(m, h, core, True) * 2 + core), device_id_type=MESH,
        )

    def share_copy(p, m):
        return pltpu.make_async_remote_copy(
            src_ref=chip_in.at[p, m], dst_ref=share_in.at[p, m],
            send_sem=share_send.at[p, m], recv_sem=share_recv.at[p, m],
            device_id=at_tile(chip * 2 + other), device_id_type=MESH,
        )

    def remote_only(m, h, act):
        if is_self(m, h):
            pl.when(core == 1)(act)
        else:
            act()

    def project(left, tiles, m, owner):
        product = jnp.dot(
            left, tile_group(tiles, m, owner, True), preferred_element_type=F32
        )
        parts = []
        for h in range(group):
            block = product[:, h * lanes : (h + 1) * lanes]
            parts.append(
                (block[:sources] * sign + swap_halves(block[sources:])).astype(BF16)
            )
        return parts

    def scatter(p, left, tiles, rank_of, ready):
        def give(m):
            for h, part in enumerate(project(left, tiles, m, other)):
                pair_out[p, m, h] = part
            if ready is None or m > 0:
                pair_copy(p, m).start()

        def keep(m):
            for h, part in enumerate(project(left, tiles, m, core)):
                pair_own[p, m, h] = part

        def finish(m):
            pair_copy(p, m).wait_recv()
            for h in range(group):
                total = pair_own[p, m, h].astype(F32) + pair_in[p, m, h].astype(F32)
                rank = rank_of(chip_at(m, h, core, True))
                total = jnp.where(rank_ids < rank, total, 0.0).astype(BF16)
                if is_self(m, h):
                    @pl.when(core == 0)
                    def _(total=total, m=m, h=h):
                        chip_in[p, m, h] = total

                def send(total=total, m=m, h=h):
                    chip_out[p, m, h] = total
                    chip_copy(p, m, h).start()

                remote_only(m, h, send)

        give(0)
        if ready is not None:
            ready()
            pair_copy(p, 0).start()
        for m in range(zc):
            if m + 1 < zc:
                give(m + 1)
            keep(m)
            finish(m)

    def stacked(coeffs):
        wide = coeffs.astype(F32)
        return jnp.concatenate([wide * sign, swap_halves(wide)], axis=0).astype(BF16)

    def expand(block, tiles, m, owner):
        left = jnp.concatenate([stacked(block[h]) for h in range(group)], axis=1)
        right = tile_group(tiles, m, owner, False)
        return lax.dot_general(
            left, right, (((1,), (1,)), ((), ())), preferred_element_type=F32
        )

    def collect(p, tiles):
        total = None
        for m in range(zc + 1):
            if m < zc:
                for h in range(group):
                    remote_only(m, h, lambda m=m, h=h: chip_copy(p, m, h).wait_recv())
                share_copy(p, m).start()
                term = expand(chip_in[p, m], tiles, m, core)
                total = term if total is None else total + term
            if m > 0:
                share_copy(p, m - 1).wait_recv()
                total = total + expand(share_in[p, m - 1], tiles, m - 1, other)
        return total

    loads[0].wait()
    start_t[...] = jnp.transpose(start_rows[...])
    loads[1].wait()
    retile(v_raw, v_tiles)

    scatter(
        0, start_t[...].astype(BF16), v_tiles,
        lambda target: ranks_ref[target, chip],
        lambda: pl.semaphore_wait(barrier, zc * group + bands - 1 + core),
    )
    loads[3].wait()
    retile(u_raw, u_tiles)
    loads[2].wait()
    observed_t = jnp.transpose(observed_rows[...])
    misfit = collect(0, u_tiles) - observed_t
    scatter(
        1, misfit.astype(BF16), u_tiles,
        lambda target: ranks_ref[chip, target],
        None,
    )
    estimate = start_t[...] - STEP_SIZE * collect(1, v_tiles)

    def band_copy(p, k):
        target = lax.rem(band + k, bands)
        src, dst = ((band_out, band_in), (thin_out_buf, thin_in))[p]
        return pltpu.make_async_remote_copy(
            src_ref=src.at[target], dst_ref=dst.at[band],
            send_sem=band_send.at[p, k], recv_sem=band_recv.at[p, k],
            device_id={"freq": target}, device_id_type=MESH,
        )

    def band_arrival(p, k):
        source = lax.rem(band + bands - k, bands)
        src, dst = ((band_out, band_in), (thin_out_buf, thin_in))[p]
        return pltpu.make_async_remote_copy(
            src_ref=src.at[source], dst_ref=dst.at[source],
            send_sem=band_send.at[p, k], recv_sem=band_recv.at[p, k],
            device_id={"freq": source}, device_id_type=MESH,
        )

    band_order = [k for k in far_first(bands) if k > 0]
    for q in range(bands):
        low = q * per_band
        slab = jnp.concatenate(
            [estimate[low : low + per_band], estimate[sources + low : sources + low + per_band]],
            axis=0,
        )
        band_out[q] = slab.astype(band_out.dtype)
    for k in band_order:
        band_copy(0, k).start()
    band_in[band] = band_out[band]
    for k in band_order:
        band_arrival(0, k).wait_recv()

    scale = 1.0 / math.sqrt(bands)
    slabs = [band_in[f].astype(F32) for f in range(bands)]
    reals = [slab[:per_band] for slab in slabs]
    imags = [slab[per_band:] for slab in slabs]
    reals, imags = small_dft(reals, imags, 1.0)
    reals = [thin_out(value * scale) for value in reals]
    imags = [thin_out(value * scale) for value in imags]
    reals, imags = small_dft(reals, imags, -1.0)
    for f in range(bands):
        slab = jnp.concatenate([reals[f], imags[f]], axis=0) * scale
        thin_out_buf[f] = slab.astype(thin_out_buf.dtype)
    for k in band_order:
        band_copy(1, k).start()
    thin_in[band] = thin_out_buf[band]
    for k in band_order:
        band_arrival(1, k).wait_recv()
    for q in range(bands):
        slab = thin_in[q].astype(F32)
        low = q * per_band
        out_ref[low : low + per_band, :] = slab[:per_band]
        out_ref[sources + low : sources + low + per_band, :] = slab[per_band:]

    for p in range(2):
        for m in range(zc):
            pair_copy(p, m).wait_send()
            share_copy(p, m).wait_send()
            for h in range(group):
                remote_only(m, h, lambda m=m, h=h: chip_copy(p, m, h).wait_send())
        for k in band_order:
            band_copy(p, k).wait_send()


def body(u_factors, v_factors, ranks, observed, start):
    zc, xc = PLANE
    bands = BANDS
    _, rows, tiles, lanes = u_factors.shape
    width = start.shape[2]
    group = xc // 2
    sources = width // 2
    per_band = sources // bands
    any_spec = pl.BlockSpec(memory_space=pl.ANY)
    block = (2, zc, group, sources, lanes)
    band_block = (bands, 2 * per_band, rows)
    result = pl.pallas_call(
        kernel,
        out_shape=jax.ShapeDtypeStruct((width, rows), F32),
        in_specs=[pl.BlockSpec(memory_space=pltpu.SMEM)] + [any_spec] * 4,
        out_specs=pl.BlockSpec(memory_space=pltpu.VMEM),
        scratch_shapes=[
            pltpu.VMEM((rows, tiles, lanes), BF16),
            pltpu.VMEM((rows, tiles, lanes), BF16),
            pltpu.VMEM((tiles, rows, lanes), BF16),
            pltpu.VMEM((tiles, rows, lanes), BF16),
            pltpu.VMEM((rows, width), F32),
            pltpu.VMEM((rows, width), F32),
            pltpu.VMEM((width, rows), F32),
            pltpu.VMEM(block, BF16),
            pltpu.VMEM(block, BF16),
            pltpu.VMEM(block, BF16),
            pltpu.VMEM(block, BF16),
            pltpu.VMEM(block, BF16),
            pltpu.VMEM(block, BF16),
            pltpu.VMEM(band_block, F32),
            pltpu.VMEM(band_block, F32),
            pltpu.VMEM(band_block, F32),
            pltpu.VMEM(band_block, F32),
            pltpu.SemaphoreType.DMA((4,)),
            pltpu.SemaphoreType.DMA((2, zc)),
            pltpu.SemaphoreType.DMA((2, zc)),
            pltpu.SemaphoreType.DMA((2, zc, group)),
            pltpu.SemaphoreType.DMA((2, zc, group)),
            pltpu.SemaphoreType.DMA((2, zc)),
            pltpu.SemaphoreType.DMA((2, zc)),
            pltpu.SemaphoreType.DMA((2, bands)),
            pltpu.SemaphoreType.DMA((2, bands)),
        ],
        compiler_params=pltpu.CompilerParams(collective_id=0, has_side_effects=True),
        name="tile_low_rank_step",
    )(ranks[0], u_factors[0], v_factors[0], observed[0], start[0])
    return jnp.transpose(result)[None]


def solution(mesh):
    in_specs = (
        P("freq", "tile", None, None),
        P("freq", "tile", None, None),
        P("freq", None, None),
        P("freq", "tile", None),
        P("freq", "tile", None),
    )
    out_specs = P("freq", "tile", None)
    return jax.shard_map(body, mesh=mesh, in_specs=in_specs, out_specs=out_specs, check_vma=False)
```

```python
import contextlib
import math

import jax
import jax.numpy as jnp
from jax import lax
from jax.experimental import pallas as pl
from jax.experimental.pallas import tpu as pltpu
from jax.sharding import PartitionSpec as P

STEP_SIZE = 0.2
LEVEL = 0.5
PLANE = (8, 4)
BANDS = 8
MESH = pl.DeviceIdType.MESH
BF16 = jnp.bfloat16
F32 = jnp.float32
SPAN = 4
EDGES = (0, 5, 8)
LOADS = 4
WIRE_FORTH = BF16
WIRE_BACK = BF16


def section(name):
    return contextlib.nullcontext()


def far_first(extent):
    order = sorted(range(extent), key=lambda d: (-min(d, extent - d), d))
    return order


def twiddle_pair(real, imag, cosine, sine):
    if abs(sine) < 1e-9:
        return (real, imag) if cosine > 0 else (-real, -imag)
    if abs(cosine) < 1e-9:
        return (-imag, real) if sine > 0 else (imag, -real)
    return real * cosine - imag * sine, real * sine + imag * cosine


def small_dft(reals, imags, sign):
    count = len(reals)
    if count == 1:
        return reals, imags
    even_re, even_im = small_dft(reals[0::2], imags[0::2], sign)
    odd_re, odd_im = small_dft(reals[1::2], imags[1::2], sign)
    out_re, out_im = [None] * count, [None] * count
    half = count // 2
    for k in range(half):
        angle = sign * 2.0 * math.pi * k / count
        tr, ti = twiddle_pair(odd_re[k], odd_im[k], math.cos(angle), math.sin(angle))
        out_re[k], out_im[k] = even_re[k] + tr, even_im[k] + ti
        out_re[k + half], out_im[k + half] = even_re[k] - tr, even_im[k] - ti
    return out_re, out_im


def thin_out(values):
    return values - jnp.clip(values, -LEVEL, LEVEL)


def kernel(
    ranks_ref, u_hbm, v_hbm, observed_hbm, start_hbm, out_ref,
    u_raw, v_raw, u_tiles, v_tiles, observed_rows, start_rows, start_t, total_ref,
    pair_out, pair_own, pair_in, chip_out, chip_in, share_in,
    start_out, start_in, band_out, band_in, thin_out_buf, thin_in,
    load_sem, sent, pair_recv, chip_recv, share_recv, band_recv,
):
    zc, xc = PLANE
    group = xc // 2
    bands = BANDS
    rows = u_raw.shape[0]
    lanes = u_raw.shape[2]
    rank_half = lanes // 2
    sources2 = start_t.shape[0]
    sources = sources2 // 2
    per_band = sources // bands

    place = lax.axis_index("tile")
    band = lax.axis_index("freq")
    chip = lax.div(place, 2)
    core = lax.rem(place, 2)
    other = 1 - core
    z = lax.div(chip, xc)
    x = lax.rem(chip, xc)
    order = far_first(zc)
    span = min(SPAN, zc)
    edges = sorted({min(edge, zc) for edge in EDGES})
    steps = len(edges) - 1
    batch_of = [c for c in range(steps) for _ in range(edges[c], edges[c + 1])]
    blocks = zc * group
    self_block = order.index(0) * group

    def shift_of(m, h, owner):
        return 2 * h + lax.rem(owner + order[m], 2)

    def chip_at(m, h, owner, forward):
        dz, dx = order[m], shift_of(m, h, owner)
        if forward:
            return lax.rem(z + dz, zc) * xc + lax.rem(x + dx, xc)
        return lax.rem(z + zc - dz, zc) * xc + lax.rem(x + xc - dx, xc)

    def is_self(m, h):
        return order[m] == 0 and h == 0

    def at_tile(index):
        return {"tile": index}

    barrier = pltpu.get_barrier_semaphore()

    def hail(device):
        pl.semaphore_signal(barrier, inc=1, device_id=device, device_id_type=MESH)

    def hail_all():
        for m in range(zc):
            for h in range(group):
                target = chip_at(m, h, core, True) * 2 + core
                if is_self(m, h):
                    pl.when(core == 1)(lambda target=target: hail(at_tile(target)))
                else:
                    hail(at_tile(target))
        hail(at_tile(chip * 2 + other))
        for k in range(1, bands):
            hail({"freq": lax.rem(band + k, bands)})

    chunk = rows // LOADS

    def chunk_load(source, target, c):
        part = pl.ds(c * chunk, chunk)
        return pltpu.make_async_copy(source.at[part], target.at[part], load_sem.at[c])

    v_loads = [chunk_load(v_hbm, v_raw, c) for c in range(LOADS)]
    u_load = pltpu.make_async_copy(u_hbm, u_raw, load_sem.at[LOADS])
    start_load = pltpu.make_async_copy(start_hbm, start_rows, load_sem.at[LOADS + 1])
    observed_load = pltpu.make_async_copy(observed_hbm, observed_rows, load_sem.at[LOADS + 2])
    hail_all()
    start_load.start()
    for load in v_loads:
        load.start()
    u_load.start()
    observed_load.start()

    def retile(raw, tiles, arrivals):
        def step(b, carry):
            at = pl.multiple_of(b * 16, 16)
            tiles[:, pl.ds(at, 16), :] = jnp.swapaxes(raw[pl.ds(at, 16)], 0, 1)
            return carry

        piece = rows // 16 // len(arrivals)
        for c, load in enumerate(arrivals):
            load.wait()
            lax.fori_loop(c * piece, (c + 1) * piece, step, 0)

    lane_ids = lax.broadcasted_iota(jnp.int32, (sources, lanes), 1)
    upper = lane_ids < rank_half
    rank_ids = jnp.where(upper, lane_ids, lane_ids - rank_half)
    sign = jnp.where(upper, 1.0, -1.0).astype(F32)

    def swap_halves(values):
        return jnp.concatenate([values[:, rank_half:], values[:, :rank_half]], axis=1)

    def tile_group(tiles, m, owner, forward):
        return jnp.concatenate(
            [tiles[chip_at(m, h, owner, forward)] for h in range(group)], axis=1
        )

    def pair_copy(p, c):
        part = pl.ds(c * span * group, span * group)
        return pltpu.make_async_remote_copy(
            src_ref=pair_out.at[p, part], dst_ref=pair_in.at[p, part],
            send_sem=sent.at[0], recv_sem=pair_recv.at[p, c],
            device_id=at_tile(chip * 2 + other), device_id_type=MESH,
        )

    def chip_copy(p, m, h):
        block = m * group + h
        return pltpu.make_async_remote_copy(
            src_ref=chip_out.at[p * blocks + block], dst_ref=chip_in.at[p, block],
            send_sem=sent.at[1], recv_sem=chip_recv.at[p, batch_of[m]],
            device_id=at_tile(chip_at(m, h, core, True) * 2 + core), device_id_type=MESH,
        )

    def share_copy(p, c):
        part = pl.ds(edges[c] * group, (edges[c + 1] - edges[c]) * group)
        return pltpu.make_async_remote_copy(
            src_ref=chip_in.at[p, part], dst_ref=share_in.at[p, part],
            send_sem=sent.at[2], recv_sem=share_recv.at[p, c],
            device_id=at_tile(chip * 2 + other), device_id_type=MESH,
        )

    def arrived(target, sem):
        pltpu.make_async_remote_copy(
            src_ref=target, dst_ref=target, send_sem=sent.at[0], recv_sem=sem,
            device_id=at_tile(chip * 2 + other), device_id_type=MESH,
        ).wait_recv()

    def departed(source, sem):
        pltpu.make_async_remote_copy(
            src_ref=source, dst_ref=source, send_sem=sem, recv_sem=band_recv.at[0],
            device_id=at_tile(chip * 2 + other), device_id_type=MESH,
        ).wait_send()

    def chips_arrived(p, c):
        first, count = edges[c] * group, (edges[c + 1] - edges[c]) * group
        sem = chip_recv.at[p, c]
        if first <= self_block < first + count:
            @pl.when(core == 0)
            def _():
                if count > 1:
                    arrived(chip_in.at[p, pl.ds(first, count - 1)], sem)

            @pl.when(core == 1)
            def _():
                arrived(chip_in.at[p, pl.ds(first, count)], sem)
        else:
            arrived(chip_in.at[p, pl.ds(first, count)], sem)

    def remote_only(m, h, act):
        if is_self(m, h):
            pl.when(core == 1)(act)
        else:
            act()

    def project(left, tiles, m, owner):
        product = jnp.dot(
            left, tile_group(tiles, m, owner, True), preferred_element_type=F32
        )
        parts = []
        for h in range(group):
            block = product[:, h * lanes : (h + 1) * lanes]
            parts.append(
                (block[:sources] * sign + swap_halves(block[sources:])).astype(BF16)
            )
        return parts

    chunks = range(zc // span)

    def scatter(p, left, tiles, rank_of, ready):
        def fill(target, owner, c):
            for m in range(c * span, (c + 1) * span):
                for h, part in enumerate(project(left, tiles, m, owner)):
                    target[p, m * group + h] = part

        def finish(m):
            for h in range(group):
                block = m * group + h
                total = pair_own[p, block].astype(F32) + pair_in[p, block].astype(F32)
                rank = rank_of(chip_at(m, h, core, True))
                total = jnp.where(rank_ids < rank, total, 0.0).astype(BF16)
                chip_out[p * blocks + block] = total
                if is_self(m, h):
                    @pl.when(core == 0)
                    def _(total=total, block=block):
                        chip_in[p, block] = total

        with section("give%d" % p):
            for c in chunks:
                fill(pair_out, other, c)
                if ready is None:
                    pair_copy(p, c).start()
        if ready is not None:
            with section("keep%d" % p):
                for c in chunks:
                    fill(pair_own, core, c)
            with section("ready"):
                ready()
            for c in chunks:
                pair_copy(p, c).start()
        for c in chunks:
            if ready is None:
                with section("keep%d_%d" % (p, c)):
                    fill(pair_own, core, c)
            with section("pairwait%d_%d" % (p, c)):
                pair_copy(p, c).wait_recv()
            with section("finish%d_%d" % (p, c)):
                for m in range(c * span, (c + 1) * span):
                    finish(m)
                    for h in range(group):
                        remote_only(m, h, lambda m=m, h=h: chip_copy(p, m, h).start())

    def stacked(coeffs):
        wide = coeffs.astype(F32)
        return jnp.concatenate([wide * sign, swap_halves(wide)], axis=0).astype(BF16)

    def expand(block, tiles, m, owner):
        left = jnp.concatenate([stacked(part) for part in block], axis=1)
        right = tile_group(tiles, m, owner, False)
        return lax.dot_general(
            left, right, (((1,), (1,)), ((), ())), preferred_element_type=F32
        )

    def collect(p, tiles):
        def terms(source, c, owner):
            total = None
            for m in range(edges[c], edges[c + 1]):
                block = [source[p, m * group + h] for h in range(group)]
                term = expand(block, tiles, m, owner)
                total = term if total is None else total + term
            return total

        for c in range(steps + 1):
            if c < steps:
                with section("chipwait%d_%d" % (p, c)):
                    chips_arrived(p, c)
                share_copy(p, c).start()
                with section("expand%d_%d" % (p, c)):
                    term = terms(chip_in, c, core)
                    total_ref[...] = term if c == 0 else total_ref[...] + term
            if c > 0:
                with section("sharewait%d_%d" % (p, c - 1)):
                    share_copy(p, c - 1).wait_recv()
                with section("shared%d_%d" % (p, c - 1)):
                    term = total_ref[...] + terms(share_in, c - 1, other)
                    if c < steps:
                        total_ref[...] = term
        return term

    wires = ((band_out, band_in), (thin_out_buf, thin_in), (start_out, start_in))

    def band_copy(p, k):
        target = lax.rem(band + k, bands)
        src, dst = wires[p]
        return pltpu.make_async_remote_copy(
            src_ref=src.at[target], dst_ref=dst.at[band],
            send_sem=sent.at[3 + p], recv_sem=band_recv.at[p],
            device_id={"freq": target}, device_id_type=MESH,
        )

    band_order = [k for k in far_first(bands) if k > 0]

    def to_slabs(values, target):
        for q in range(bands):
            low = q * per_band
            slab = jnp.concatenate(
                [values[low : low + per_band], values[sources + low : sources + low + per_band]],
                axis=0,
            )
            target[q] = slab.astype(target.dtype)

    with section("start"):
        start_load.wait()
        start_t[...] = jnp.transpose(start_rows[...])
        to_slabs(start_t[...], start_out)
        start_in[band] = start_out[band]
    with section("retile_v"):
        retile(v_raw, v_tiles, v_loads)
    scatter(
        0, start_t[...].astype(BF16), v_tiles,
        lambda target: ranks_ref[target, chip],
        lambda: pl.semaphore_wait(barrier, zc * group + bands - 1 + core),
    )
    for k in band_order:
        band_copy(2, k).start()
    with section("retile_u"):
        retile(u_raw, u_tiles, [u_load])
        observed_load.wait()
        observed_t = jnp.transpose(observed_rows[...])
    misfit = collect(0, u_tiles) - observed_t
    scatter(
        1, misfit.astype(BF16), u_tiles,
        lambda target: ranks_ref[chip, target],
        None,
    )
    change = -STEP_SIZE * collect(1, v_tiles)

    to_slabs(change, band_out)
    for k in band_order:
        band_copy(0, k).start()
    band_in[band] = band_out[band]
    with section("bandwait0"):
        arrived(start_in.at[pl.ds(0, bands - 1)], band_recv.at[2])
        arrived(band_in.at[pl.ds(0, bands - 1)], band_recv.at[0])

    scale = 1.0 / math.sqrt(bands)
    slabs = [start_in[f] + band_in[f].astype(F32) for f in range(bands)]
    reals = [slab[:per_band] for slab in slabs]
    imags = [slab[per_band:] for slab in slabs]
    reals, imags = small_dft(reals, imags, 1.0)
    reals = [thin_out(value * scale) for value in reals]
    imags = [thin_out(value * scale) for value in imags]
    reals, imags = small_dft(reals, imags, -1.0)
    for f in range(bands):
        slab = jnp.concatenate([reals[f], imags[f]], axis=0) * scale
        thin_out_buf[f] = slab.astype(thin_out_buf.dtype)
    for k in band_order:
        band_copy(1, k).start()
    thin_in[band] = thin_out_buf[band]
    with section("bandwait1"):
        arrived(thin_in.at[pl.ds(0, bands - 1)], band_recv.at[1])
    with section("out"):
        slabs = [thin_in[q].astype(F32) for q in range(bands)]
        whole = jnp.concatenate(
            [slab[:per_band] for slab in slabs] + [slab[per_band:] for slab in slabs], axis=0
        )
        out_ref[...] = jnp.transpose(whole)

    with section("tail"):
        departed(pair_out, sent.at[0])
        departed(chip_in, sent.at[2])
        for p in range(3):
            departed(wires[p][0].at[pl.ds(0, bands - 1)], sent.at[3 + p])

        @pl.when(core == 0)
        def _():
            departed(chip_out.at[pl.ds(0, 2 * blocks - 2)], sent.at[1])

        @pl.when(core == 1)
        def _():
            departed(chip_out, sent.at[1])


def body(u_factors, v_factors, ranks, observed, start):
    zc, xc = PLANE
    bands = BANDS
    _, rows, tiles, lanes = u_factors.shape
    width = start.shape[2]
    group = xc // 2
    sources = width // 2
    per_band = sources // bands
    any_spec = pl.BlockSpec(memory_space=pl.ANY)
    block = (2, zc * group, sources, lanes)
    band_block = (bands, 2 * per_band, rows)
    result = pl.pallas_call(
        kernel,
        out_shape=pltpu.MemorySpace.VMEM((rows, width), F32),
        in_specs=[pl.BlockSpec(memory_space=pltpu.SMEM)] + [any_spec] * 4,
        out_specs=pl.BlockSpec(memory_space=pltpu.VMEM),
        scratch_shapes=[
            pltpu.VMEM((rows, tiles, lanes), BF16),
            pltpu.VMEM((rows, tiles, lanes), BF16),
            pltpu.VMEM((tiles, rows, lanes), BF16),
            pltpu.VMEM((tiles, rows, lanes), BF16),
            pltpu.VMEM((rows, width), F32),
            pltpu.VMEM((rows, width), F32),
            pltpu.VMEM((width, rows), F32),
            pltpu.VMEM((width, rows), F32),
            pltpu.VMEM(block, BF16),
            pltpu.VMEM(block, BF16),
            pltpu.VMEM(block, BF16),
            pltpu.VMEM((2 * zc * group, sources, lanes), BF16),
            pltpu.VMEM(block, BF16),
            pltpu.VMEM(block, BF16),
            pltpu.VMEM(band_block, F32),
            pltpu.VMEM(band_block, F32),
            pltpu.VMEM(band_block, WIRE_FORTH),
            pltpu.VMEM(band_block, WIRE_FORTH),
            pltpu.VMEM(band_block, WIRE_BACK),
            pltpu.VMEM(band_block, WIRE_BACK),
            pltpu.SemaphoreType.DMA((LOADS + 3,)),
            pltpu.SemaphoreType.DMA((6,)),
            pltpu.SemaphoreType.DMA((2, max(zc // SPAN, 1))),
            pltpu.SemaphoreType.DMA((2, len(EDGES))),
            pltpu.SemaphoreType.DMA((2, len(EDGES))),
            pltpu.SemaphoreType.DMA((3,)),
        ],
        compiler_params=pltpu.CompilerParams(collective_id=0, has_side_effects=True),
        name="tile_low_rank_step",
    )(ranks[0], u_factors[0], v_factors[0], observed[0], start[0])
    return result[None]


def solution(mesh):
    in_specs = (
        P("freq", "tile", None, None),
        P("freq", "tile", None, None),
        P("freq", None, None),
        P("freq", "tile", None),
        P("freq", "tile", None),
    )
    out_specs = P("freq", "tile", None)
    return jax.shard_map(body, mesh=mesh, in_specs=in_specs, out_specs=out_specs, check_vma=False)
```

```python
import contextlib
import math

import jax
import jax.numpy as jnp
from jax import lax
from jax.experimental import pallas as pl
from jax.experimental.pallas import tpu as pltpu
from jax.sharding import PartitionSpec as P

STEP_SIZE = 0.2
LEVEL = 0.5
PLANE = (8, 4)
BANDS = 8
MESH = pl.DeviceIdType.MESH
BF16 = jnp.bfloat16
F32 = jnp.float32
SPAN = 4
STRIDE = 4
EDGES = (0, 4, 8)
LOADS = 4
WIRE_FORTH = BF16
WIRE_BACK = BF16


def section(name):
    return contextlib.nullcontext()


def far_first(extent):
    order = sorted(range(extent), key=lambda d: (-min(d, extent - d), d))
    return order


def twiddle_pair(real, imag, cosine, sine):
    if abs(sine) < 1e-9:
        return (real, imag) if cosine > 0 else (-real, -imag)
    if abs(cosine) < 1e-9:
        return (-imag, real) if sine > 0 else (imag, -real)
    return real * cosine - imag * sine, real * sine + imag * cosine


def small_dft(reals, imags, sign):
    count = len(reals)
    if count == 1:
        return reals, imags
    even_re, even_im = small_dft(reals[0::2], imags[0::2], sign)
    odd_re, odd_im = small_dft(reals[1::2], imags[1::2], sign)
    out_re, out_im = [None] * count, [None] * count
    half = count // 2
    for k in range(half):
        angle = sign * 2.0 * math.pi * k / count
        tr, ti = twiddle_pair(odd_re[k], odd_im[k], math.cos(angle), math.sin(angle))
        out_re[k], out_im[k] = even_re[k] + tr, even_im[k] + ti
        out_re[k + half], out_im[k + half] = even_re[k] - tr, even_im[k] - ti
    return out_re, out_im


def thin_out(values):
    return values - jnp.clip(values, -LEVEL, LEVEL)


def kernel(
    ranks_ref, u_hbm, v_hbm, observed_hbm, start_hbm, out_ref,
    u_raw, v_raw, u_tiles, v_tiles, observed_rows, start_rows, start_t, total_ref,
    u_far, image_out, image_in,
    pair_out, pair_own, pair_in, chip_out, chip_in, share_in,
    start_out, start_in, band_out, band_in, thin_out_buf, thin_in,
    load_sem, sent, pair_recv, chip_recv, share_recv, band_recv, far_recv, image_recv,
):
    zc, xc = PLANE
    group = xc // 2
    bands = BANDS
    rows = u_raw.shape[0]
    lanes = u_raw.shape[2]
    rank_half = lanes // 2
    sources2 = start_t.shape[0]
    sources = sources2 // 2
    per_band = sources // bands

    place = lax.axis_index("tile")
    band = lax.axis_index("freq")
    chip = lax.div(place, 2)
    core = lax.rem(place, 2)
    other = 1 - core
    z = lax.div(chip, xc)
    x = lax.rem(chip, xc)
    order = far_first(zc)
    span, stride = min(SPAN, zc), min(STRIDE, zc)
    edges = sorted({min(edge, zc) for edge in EDGES})
    steps = len(edges) - 1
    batch_of = [c for c in range(steps) for _ in range(edges[c], edges[c + 1])]
    blocks = zc * group
    self_block = order.index(0) * group

    def shift_of(m, h, owner):
        return 2 * h + lax.rem(owner + order[m], 2)

    def chip_at(m, h, owner, forward):
        dz, dx = order[m], shift_of(m, h, owner)
        if forward:
            return lax.rem(z + dz, zc) * xc + lax.rem(x + dx, xc)
        return lax.rem(z + zc - dz, zc) * xc + lax.rem(x + xc - dx, xc)

    def is_self(m, h):
        return order[m] == 0 and h == 0

    def at_tile(index):
        return {"tile": index}

    barrier = pltpu.get_barrier_semaphore()

    def hail(device):
        pl.semaphore_signal(barrier, inc=1, device_id=device, device_id_type=MESH)

    def hail_all():
        for m in range(zc):
            for h in range(group):
                target = chip_at(m, h, core, True) * 2 + core
                if is_self(m, h):
                    pl.when(core == 1)(lambda target=target: hail(at_tile(target)))
                else:
                    hail(at_tile(target))
        hail(at_tile(chip * 2 + other))
        for k in range(1, bands):
            hail({"freq": lax.rem(band + k, bands)})

    chunk = rows // LOADS

    def chunk_load(source, target, c):
        part = pl.ds(c * chunk, chunk)
        return pltpu.make_async_copy(source.at[part], target.at[part], load_sem.at[c])

    v_loads = [chunk_load(v_hbm, v_raw, c) for c in range(LOADS)]
    u_load = pltpu.make_async_copy(u_hbm, u_raw, load_sem.at[LOADS])
    start_load = pltpu.make_async_copy(start_hbm, start_rows, load_sem.at[LOADS + 1])
    observed_load = pltpu.make_async_copy(observed_hbm, observed_rows, load_sem.at[LOADS + 2])
    hail_all()
    start_load.start()
    for load in v_loads:
        load.start()
    u_load.start()
    observed_load.start()

    def retile(raw, tiles, arrivals):
        def step(b, carry):
            at = pl.multiple_of(b * 16, 16)
            tiles[:, pl.ds(at, 16), :] = jnp.swapaxes(raw[pl.ds(at, 16)], 0, 1)
            return carry

        piece = rows // 16 // len(arrivals)
        for c, load in enumerate(arrivals):
            load.wait()
            lax.fori_loop(c * piece, (c + 1) * piece, step, 0)

    lane_ids = lax.broadcasted_iota(jnp.int32, (sources, lanes), 1)
    upper = lane_ids < rank_half
    rank_ids = jnp.where(upper, lane_ids, lane_ids - rank_half)
    sign = jnp.where(upper, 1.0, -1.0).astype(F32)

    def swap_halves(values):
        return jnp.concatenate([values[:, rank_half:], values[:, :rank_half]], axis=1)

    def tile_group(tiles, m, owner, forward):
        return jnp.concatenate(
            [tiles[chip_at(m, h, owner, forward)] for h in range(group)], axis=1
        )

    def far_group(m, forward):
        return jnp.concatenate(
            [u_far[lax.div(chip_at(m, h, core, forward), 2)] for h in range(group)], axis=1
        )

    def pair_copy(c):
        part = pl.ds(c * span * group, span * group)
        return pltpu.make_async_remote_copy(
            src_ref=pair_out.at[part], dst_ref=pair_in.at[part],
            send_sem=sent.at[0], recv_sem=pair_recv.at[c],
            device_id=at_tile(chip * 2 + other), device_id_type=MESH,
        )

    def chip_copy(p, m, h):
        block = m * group + h
        return pltpu.make_async_remote_copy(
            src_ref=chip_out.at[p * blocks + block], dst_ref=chip_in.at[p, block],
            send_sem=sent.at[1], recv_sem=chip_recv.at[p, batch_of[m]],
            device_id=at_tile(chip_at(m, h, core, True) * 2 + core), device_id_type=MESH,
        )

    def share_copy(c):
        part = pl.ds(edges[c] * group, (edges[c + 1] - edges[c]) * group)
        return pltpu.make_async_remote_copy(
            src_ref=chip_in.at[1, part], dst_ref=share_in.at[part],
            send_sem=sent.at[2], recv_sem=share_recv.at[c],
            device_id=at_tile(chip * 2 + other), device_id_type=MESH,
        )

    def far_copy(m, h):
        tile = chip_at(m, h, other, True)
        return pltpu.make_async_remote_copy(
            src_ref=u_tiles.at[tile], dst_ref=u_far.at[lax.div(tile, 2)],
            send_sem=sent.at[6], recv_sem=far_recv.at[0],
            device_id=at_tile(chip * 2 + other), device_id_type=MESH,
        )

    def image_copy(half):
        return pltpu.make_async_remote_copy(
            src_ref=image_out.at[half], dst_ref=image_in.at[1 - half],
            send_sem=sent.at[7], recv_sem=image_recv.at[1 - half],
            device_id=at_tile(chip * 2 + other), device_id_type=MESH,
        )

    def arrived(target, sem):
        pltpu.make_async_remote_copy(
            src_ref=target, dst_ref=target, send_sem=sent.at[0], recv_sem=sem,
            device_id=at_tile(chip * 2 + other), device_id_type=MESH,
        ).wait_recv()

    def departed(source, sem):
        pltpu.make_async_remote_copy(
            src_ref=source, dst_ref=source, send_sem=sem, recv_sem=band_recv.at[0],
            device_id=at_tile(chip * 2 + other), device_id_type=MESH,
        ).wait_send()

    def chips_arrived(p, c):
        first, count = edges[c] * group, (edges[c + 1] - edges[c]) * group
        sem = chip_recv.at[p, c]
        if first <= self_block < first + count:
            @pl.when(core == 0)
            def _():
                if count > 1:
                    arrived(chip_in.at[p, pl.ds(first, count - 1)], sem)

            @pl.when(core == 1)
            def _():
                arrived(chip_in.at[p, pl.ds(first, count)], sem)
        else:
            arrived(chip_in.at[p, pl.ds(first, count)], sem)

    def remote_only(m, h, act):
        if is_self(m, h):
            pl.when(core == 1)(act)
        else:
            act()

    def project(left, right):
        product = jnp.dot(left, right, preferred_element_type=F32)
        parts = []
        for h in range(group):
            block = product[:, h * lanes : (h + 1) * lanes]
            parts.append(block[:sources] * sign + swap_halves(block[sources:]))
        return parts

    def masked(part, rank):
        return jnp.where(rank_ids < rank, part, 0.0).astype(BF16)

    def post(p, m, parts):
        for h, part in enumerate(parts):
            block = m * group + h
            chip_out[p * blocks + block] = part
            if is_self(m, h):
                @pl.when(core == 0)
                def _(part=part, block=block):
                    chip_in[p, block] = part

        for h in range(group):
            remote_only(m, h, lambda m=m, h=h: chip_copy(p, m, h).start())

    chunks = range(zc // span)

    def scatter_first(left, ready):
        def fill(target, owner):
            for m in range(zc):
                for h, part in enumerate(project(left, tile_group(v_tiles, m, owner, True))):
                    target[m * group + h] = part.astype(BF16)

        with section("give0"):
            fill(pair_out, other)
        with section("keep0"):
            fill(pair_own, core)
        with section("ready"):
            ready()
        for c in chunks:
            pair_copy(c).start()
        for c in chunks:
            with section("pairwait0_%d" % c):
                pair_copy(c).wait_recv()
            with section("finish0_%d" % c):
                for m in range(c * span, (c + 1) * span):
                    parts = []
                    for h in range(group):
                        block = m * group + h
                        total = pair_own[block].astype(F32) + pair_in[block].astype(F32)
                        parts.append(masked(total, ranks_ref[chip_at(m, h, core, True), chip]))
                    post(0, m, parts)

    def scatter_second(left):
        for c in range(zc // stride):
            with section("project1_%d" % c):
                ready = []
                for m in range(c * stride, (c + 1) * stride):
                    right = jnp.concatenate(
                        [tile_group(u_tiles, m, core, True), far_group(m, True)], axis=0
                    )
                    ready.append([
                        masked(part, ranks_ref[chip, chip_at(m, h, core, True)])
                        for h, part in enumerate(project(left, right))
                    ])
                for i, parts in enumerate(ready):
                    post(1, c * stride + i, parts)

    def stacked(coeffs):
        wide = coeffs.astype(F32)
        return jnp.concatenate([wide * sign, swap_halves(wide)], axis=0).astype(BF16)

    def expand(left, right):
        return lax.dot_general(
            left, right, (((1,), (1,)), ((), ())), preferred_element_type=F32
        )

    def gathered(block):
        return jnp.concatenate([stacked(part) for part in block], axis=1)

    def collect_first():
        for c in range(steps):
            with section("chipwait0_%d" % c):
                chips_arrived(0, c)
                if c == 0:
                    arrived(u_far, far_recv.at[0])
            with section("expand0_%d" % c):
                members = range(edges[c], edges[c + 1])
                lefts = [gathered([chip_in[0, m * group + h] for h in range(group)]) for m in members]
                for half in (1, 0):
                    total = None if c == 0 and half else image_out[half]
                    for m, left in zip(members, lefts):
                        right = far_group(m, False) if half else tile_group(u_tiles, m, core, False)
                        term = expand(left, right)
                        total = term if total is None else total + term
                    image_out[half] = total
                    if c == steps - 1:
                        image_copy(half).start()
        with section("imagewait"):
            for half in (0, 1):
                image_copy(1 - half).wait_recv()
        return jnp.concatenate([image_out[half] + image_in[half] for half in (0, 1)], axis=1)

    def collect_second():
        def terms(source, c, owner):
            total = None
            for m in range(edges[c], edges[c + 1]):
                left = gathered([source[m * group + h] for h in range(group)])
                term = expand(left, tile_group(v_tiles, m, owner, False))
                total = term if total is None else total + term
            return total

        for c in range(steps + 1):
            if c < steps:
                with section("chipwait1_%d" % c):
                    chips_arrived(1, c)
                share_copy(c).start()
                with section("expand1_%d" % c):
                    term = terms(chip_in.at[1], c, core)
                    total_ref[...] = term if c == 0 else total_ref[...] + term
            if c > 0:
                with section("sharewait1_%d" % (c - 1)):
                    share_copy(c - 1).wait_recv()
                with section("shared1_%d" % (c - 1)):
                    term = total_ref[...] + terms(share_in, c - 1, other)
                    if c < steps:
                        total_ref[...] = term
        return term

    wires = ((band_out, band_in), (thin_out_buf, thin_in), (start_out, start_in))

    def band_copy(p, k):
        target = lax.rem(band + k, bands)
        src, dst = wires[p]
        return pltpu.make_async_remote_copy(
            src_ref=src.at[target], dst_ref=dst.at[band],
            send_sem=sent.at[3 + p], recv_sem=band_recv.at[p],
            device_id={"freq": target}, device_id_type=MESH,
        )

    band_order = [k for k in far_first(bands) if k > 0]

    def to_slabs(values, target):
        for q in range(bands):
            low = q * per_band
            slab = jnp.concatenate(
                [values[low : low + per_band], values[sources + low : sources + low + per_band]],
                axis=0,
            )
            target[q] = slab.astype(target.dtype)

    with section("start"):
        start_load.wait()
        start_t[...] = jnp.transpose(start_rows[...])
        to_slabs(start_t[...], start_out)
        start_in[band] = start_out[band]
    with section("retile_v"):
        retile(v_raw, v_tiles, v_loads)
    scatter_first(
        start_t[...].astype(BF16),
        lambda: pl.semaphore_wait(barrier, zc * group + bands - 1 + core),
    )
    with section("retile_u"):
        retile(u_raw, u_tiles, [u_load])
        for m in range(zc):
            for h in range(group):
                far_copy(m, h).start()
        for k in band_order:
            band_copy(2, k).start()
        observed_load.wait()
        image_out[0] = -jnp.transpose(observed_rows[...])
    misfit = collect_first()
    scatter_second(misfit.astype(BF16))
    change = -STEP_SIZE * collect_second()

    to_slabs(change, band_out)
    for k in band_order:
        band_copy(0, k).start()
    band_in[band] = band_out[band]
    with section("bandwait0"):
        arrived(start_in.at[pl.ds(0, bands - 1)], band_recv.at[2])
        arrived(band_in.at[pl.ds(0, bands - 1)], band_recv.at[0])

    scale = 1.0 / math.sqrt(bands)
    slabs = [start_in[f] + band_in[f].astype(F32) for f in range(bands)]
    reals = [slab[:per_band] for slab in slabs]
    imags = [slab[per_band:] for slab in slabs]
    reals, imags = small_dft(reals, imags, 1.0)
    reals = [thin_out(value * scale) for value in reals]
    imags = [thin_out(value * scale) for value in imags]
    reals, imags = small_dft(reals, imags, -1.0)
    for f in range(bands):
        slab = jnp.concatenate([reals[f], imags[f]], axis=0) * scale
        thin_out_buf[f] = slab.astype(thin_out_buf.dtype)
    for k in band_order:
        band_copy(1, k).start()
    thin_in[band] = thin_out_buf[band]
    with section("bandwait1"):
        arrived(thin_in.at[pl.ds(0, bands - 1)], band_recv.at[1])
    with section("out"):
        slabs = [thin_in[q].astype(F32) for q in range(bands)]
        whole = jnp.concatenate(
            [slab[:per_band] for slab in slabs] + [slab[per_band:] for slab in slabs], axis=0
        )
        out_ref[...] = jnp.transpose(whole)

    with section("tail"):
        departed(pair_out, sent.at[0])
        departed(chip_in.at[1], sent.at[2])
        departed(u_far, sent.at[6])
        departed(image_out, sent.at[7])
        for p in range(3):
            departed(wires[p][0].at[pl.ds(0, bands - 1)], sent.at[3 + p])

        @pl.when(core == 0)
        def _():
            departed(chip_out.at[pl.ds(0, 2 * blocks - 2)], sent.at[1])

        @pl.when(core == 1)
        def _():
            departed(chip_out, sent.at[1])


def body(u_factors, v_factors, ranks, observed, start):
    zc, xc = PLANE
    bands = BANDS
    _, rows, tiles, lanes = u_factors.shape
    width = start.shape[2]
    group = xc // 2
    sources = width // 2
    per_band = sources // bands
    any_spec = pl.BlockSpec(memory_space=pl.ANY)
    block = (zc * group, sources, lanes)
    band_block = (bands, 2 * per_band, rows)
    result = pl.pallas_call(
        kernel,
        out_shape=pltpu.MemorySpace.VMEM((rows, width), F32),
        in_specs=[pl.BlockSpec(memory_space=pltpu.SMEM)] + [any_spec] * 4,
        out_specs=pl.BlockSpec(memory_space=pltpu.VMEM),
        scratch_shapes=[
            pltpu.VMEM((rows, tiles, lanes), BF16),
            pltpu.VMEM((rows, tiles, lanes), BF16),
            pltpu.VMEM((tiles, rows, lanes), BF16),
            pltpu.VMEM((tiles, rows, lanes), BF16),
            pltpu.VMEM((rows, width), F32),
            pltpu.VMEM((rows, width), F32),
            pltpu.VMEM((width, rows), F32),
            pltpu.VMEM((width, rows), F32),
            pltpu.VMEM((tiles // 2, rows, lanes), BF16),
            pltpu.VMEM((2, width, rows), F32),
            pltpu.VMEM((2, width, rows), F32),
            pltpu.VMEM(block, BF16),
            pltpu.VMEM(block, BF16),
            pltpu.VMEM(block, BF16),
            pltpu.VMEM((2 * zc * group, sources, lanes), BF16),
            pltpu.VMEM((2,) + block, BF16),
            pltpu.VMEM(block, BF16),
            pltpu.VMEM(band_block, F32),
            pltpu.VMEM(band_block, F32),
            pltpu.VMEM(band_block, WIRE_FORTH),
            pltpu.VMEM(band_block, WIRE_FORTH),
            pltpu.VMEM(band_block, WIRE_BACK),
            pltpu.VMEM(band_block, WIRE_BACK),
            pltpu.SemaphoreType.DMA((LOADS + 3,)),
            pltpu.SemaphoreType.DMA((8,)),
            pltpu.SemaphoreType.DMA((max(zc // SPAN, 1),)),
            pltpu.SemaphoreType.DMA((2, len(EDGES))),
            pltpu.SemaphoreType.DMA((len(EDGES),)),
            pltpu.SemaphoreType.DMA((3,)),
            pltpu.SemaphoreType.DMA((1,)),
            pltpu.SemaphoreType.DMA((2,)),
        ],
        compiler_params=pltpu.CompilerParams(collective_id=0, has_side_effects=True),
        name="tile_low_rank_step",
    )(ranks[0], u_factors[0], v_factors[0], observed[0], start[0])
    return result[None]


def solution(mesh):
    in_specs = (
        P("freq", "tile", None, None),
        P("freq", "tile", None, None),
        P("freq", None, None),
        P("freq", "tile", None),
        P("freq", "tile", None),
    )
    out_specs = P("freq", "tile", None)
    return jax.shard_map(body, mesh=mesh, in_specs=in_specs, out_specs=out_specs, check_vma=False)
```

```python
import contextlib
import math

import jax
import jax.numpy as jnp
from jax import lax
from jax.experimental import pallas as pl
from jax.experimental.pallas import tpu as pltpu
from jax.sharding import PartitionSpec as P

STEP_SIZE = 0.2
LEVEL = 0.5
PLANE = (8, 4)
BANDS = 8
MESH = pl.DeviceIdType.MESH
BF16 = jnp.bfloat16
F32 = jnp.float32
SPAN = 4
STRIDE = 4
EDGES = (0, 4, 8)
LOADS = 4
WIRE_FORTH = BF16
WIRE_BACK = BF16


def section(name):
    return contextlib.nullcontext()


def far_first(extent):
    order = sorted(range(extent), key=lambda d: (-min(d, extent - d), d))
    return order


def twiddle_pair(real, imag, cosine, sine):
    if abs(sine) < 1e-9:
        return (real, imag) if cosine > 0 else (-real, -imag)
    if abs(cosine) < 1e-9:
        return (-imag, real) if sine > 0 else (imag, -real)
    return real * cosine - imag * sine, real * sine + imag * cosine


def small_dft(reals, imags, sign):
    count = len(reals)
    if count == 1:
        return reals, imags
    even_re, even_im = small_dft(reals[0::2], imags[0::2], sign)
    odd_re, odd_im = small_dft(reals[1::2], imags[1::2], sign)
    out_re, out_im = [None] * count, [None] * count
    half = count // 2
    for k in range(half):
        angle = sign * 2.0 * math.pi * k / count
        tr, ti = twiddle_pair(odd_re[k], odd_im[k], math.cos(angle), math.sin(angle))
        out_re[k], out_im[k] = even_re[k] + tr, even_im[k] + ti
        out_re[k + half], out_im[k + half] = even_re[k] - tr, even_im[k] - ti
    return out_re, out_im


def thin_out(values):
    return values - jnp.clip(values, -LEVEL, LEVEL)


def kernel(
    ranks_hbm, u_hbm, v_hbm, observed_hbm, start_hbm, out_ref,
    ranks_ref, u_raw, v_raw, u_tiles, v_tiles, observed_rows, start_rows, start_t, total_ref,
    u_far, image_out, image_in,
    pair_out, pair_own, pair_in, chip_out, chip_in, share_in,
    start_out, start_in, band_out, band_in, thin_out_buf, thin_in,
    load_sem, sent, pair_recv, chip_recv, share_recv, band_recv, far_recv, image_recv,
):
    zc, xc = PLANE
    group = xc // 2
    bands = BANDS
    rows = u_raw.shape[0]
    lanes = u_raw.shape[2]
    rank_half = lanes // 2
    sources2 = start_t.shape[0]
    sources = sources2 // 2
    per_band = sources // bands

    place = lax.axis_index("tile")
    band = lax.axis_index("freq")
    chip = lax.div(place, 2)
    core = lax.rem(place, 2)
    other = 1 - core
    z = lax.div(chip, xc)
    x = lax.rem(chip, xc)
    order = far_first(zc)
    span, stride = min(SPAN, zc), min(STRIDE, zc)
    edges = sorted({min(edge, zc) for edge in EDGES})
    steps = len(edges) - 1
    batch_of = [c for c in range(steps) for _ in range(edges[c], edges[c + 1])]
    blocks = zc * group
    self_block = order.index(0) * group

    def shift_of(m, h, owner):
        return 2 * h + lax.rem(owner + order[m], 2)

    def chip_at(m, h, owner, forward):
        dz, dx = order[m], shift_of(m, h, owner)
        if forward:
            return lax.rem(z + dz, zc) * xc + lax.rem(x + dx, xc)
        return lax.rem(z + zc - dz, zc) * xc + lax.rem(x + xc - dx, xc)

    def is_self(m, h):
        return order[m] == 0 and h == 0

    def at_tile(index):
        return {"tile": index}

    barrier = pltpu.get_barrier_semaphore()

    def hail(device):
        pl.semaphore_signal(barrier, inc=1, device_id=device, device_id_type=MESH)

    def hail_all():
        for m in range(zc):
            for h in range(group):
                target = chip_at(m, h, core, True) * 2 + core
                if is_self(m, h):
                    pl.when(core == 1)(lambda target=target: hail(at_tile(target)))
                else:
                    hail(at_tile(target))
        hail(at_tile(chip * 2 + other))
        for k in range(1, bands):
            hail({"freq": lax.rem(band + k, bands)})

    chunk = rows // LOADS

    def chunk_load(source, target, c):
        part = pl.ds(c * chunk, chunk)
        return pltpu.make_async_copy(source.at[part], target.at[part], load_sem.at[c])

    v_loads = [chunk_load(v_hbm, v_raw, c) for c in range(LOADS)]
    u_load = pltpu.make_async_copy(u_hbm, u_raw, load_sem.at[LOADS])
    start_load = pltpu.make_async_copy(start_hbm, start_rows, load_sem.at[LOADS + 1])
    observed_load = pltpu.make_async_copy(observed_hbm, observed_rows, load_sem.at[LOADS + 2])
    hail_all()
    ranks_load = pltpu.make_async_copy(ranks_hbm, ranks_ref, load_sem.at[LOADS + 3])
    start_load.start()
    for load in v_loads:
        load.start()
    ranks_load.start()
    u_load.start()
    observed_load.start()

    def retile(raw, tiles, arrivals):
        def step(b, carry):
            at = pl.multiple_of(b * 16, 16)
            tiles[:, pl.ds(at, 16), :] = jnp.swapaxes(raw[pl.ds(at, 16)], 0, 1)
            return carry

        piece = rows // 16 // len(arrivals)
        for c, load in enumerate(arrivals):
            load.wait()
            lax.fori_loop(c * piece, (c + 1) * piece, step, 0)

    lane_ids = lax.broadcasted_iota(jnp.int32, (sources, lanes), 1)
    upper = lane_ids < rank_half
    rank_ids = jnp.where(upper, lane_ids, lane_ids - rank_half)
    sign = jnp.where(upper, 1.0, -1.0).astype(F32)

    def swap_halves(values):
        return jnp.concatenate([values[:, rank_half:], values[:, :rank_half]], axis=1)

    def tile_group(tiles, m, owner, forward):
        return jnp.concatenate(
            [tiles[chip_at(m, h, owner, forward)] for h in range(group)], axis=1
        )

    def far_group(m, forward):
        return jnp.concatenate(
            [u_far[lax.div(chip_at(m, h, core, forward), 2)] for h in range(group)], axis=1
        )

    def pair_copy(c):
        part = pl.ds(c * span * group, span * group)
        return pltpu.make_async_remote_copy(
            src_ref=pair_out.at[part], dst_ref=pair_in.at[part],
            send_sem=sent.at[0], recv_sem=pair_recv.at[c],
            device_id=at_tile(chip * 2 + other), device_id_type=MESH,
        )

    def chip_copy(p, m, h):
        block = m * group + h
        return pltpu.make_async_remote_copy(
            src_ref=chip_out.at[p * blocks + block], dst_ref=chip_in.at[p, block],
            send_sem=sent.at[1], recv_sem=chip_recv.at[p, batch_of[m]],
            device_id=at_tile(chip_at(m, h, core, True) * 2 + core), device_id_type=MESH,
        )

    def share_copy(c):
        part = pl.ds(edges[c] * group, (edges[c + 1] - edges[c]) * group)
        return pltpu.make_async_remote_copy(
            src_ref=chip_in.at[1, part], dst_ref=share_in.at[part],
            send_sem=sent.at[2], recv_sem=share_recv.at[c],
            device_id=at_tile(chip * 2 + other), device_id_type=MESH,
        )

    def far_copy(m, h):
        tile = chip_at(m, h, other, True)
        return pltpu.make_async_remote_copy(
            src_ref=u_tiles.at[tile], dst_ref=u_far.at[lax.div(tile, 2)],
            send_sem=sent.at[6], recv_sem=far_recv.at[0],
            device_id=at_tile(chip * 2 + other), device_id_type=MESH,
        )

    def image_copy(half):
        return pltpu.make_async_remote_copy(
            src_ref=image_out.at[half], dst_ref=image_in.at[1 - half],
            send_sem=sent.at[7], recv_sem=image_recv.at[1 - half],
            device_id=at_tile(chip * 2 + other), device_id_type=MESH,
        )

    def arrived(target, sem):
        pltpu.make_async_remote_copy(
            src_ref=target, dst_ref=target, send_sem=sent.at[0], recv_sem=sem,
            device_id=at_tile(chip * 2 + other), device_id_type=MESH,
        ).wait_recv()

    def departed(source, sem):
        pltpu.make_async_remote_copy(
            src_ref=source, dst_ref=source, send_sem=sem, recv_sem=band_recv.at[0],
            device_id=at_tile(chip * 2 + other), device_id_type=MESH,
        ).wait_send()

    def chips_arrived(p, c):
        first, count = edges[c] * group, (edges[c + 1] - edges[c]) * group
        sem = chip_recv.at[p, c]
        if first <= self_block < first + count:
            @pl.when(core == 0)
            def _():
                if count > 1:
                    arrived(chip_in.at[p, pl.ds(first, count - 1)], sem)

            @pl.when(core == 1)
            def _():
                arrived(chip_in.at[p, pl.ds(first, count)], sem)
        else:
            arrived(chip_in.at[p, pl.ds(first, count)], sem)

    def remote_only(m, h, act):
        if is_self(m, h):
            pl.when(core == 1)(act)
        else:
            act()

    def project(left, right):
        product = jnp.dot(left, right, preferred_element_type=F32)
        parts = []
        for h in range(group):
            block = product[:, h * lanes : (h + 1) * lanes]
            parts.append(block[:sources] * sign + swap_halves(block[sources:]))
        return parts

    def masked(part, rank):
        return jnp.where(rank_ids < rank, part, 0.0).astype(BF16)

    def post(p, m, parts):
        for h, part in enumerate(parts):
            block = m * group + h
            chip_out[p * blocks + block] = part
            if is_self(m, h):
                @pl.when(core == 0)
                def _(part=part, block=block):
                    chip_in[p, block] = part

        for h in range(group):
            remote_only(m, h, lambda m=m, h=h: chip_copy(p, m, h).start())

    chunks = range(zc // span)

    def scatter_first(left, ready):
        def fill(target, owner):
            for m in range(zc):
                for h, part in enumerate(project(left, tile_group(v_tiles, m, owner, True))):
                    target[m * group + h] = part.astype(BF16)

        with section("give0"):
            fill(pair_out, other)
        with section("keep0"):
            fill(pair_own, core)
            ranks_load.wait()
        with section("ready"):
            ready()
        for c in chunks:
            pair_copy(c).start()
        for c in chunks:
            with section("pairwait0_%d" % c):
                pair_copy(c).wait_recv()
            with section("finish0_%d" % c):
                for m in range(c * span, (c + 1) * span):
                    parts = []
                    for h in range(group):
                        block = m * group + h
                        total = pair_own[block].astype(F32) + pair_in[block].astype(F32)
                        parts.append(masked(total, ranks_ref[chip_at(m, h, core, True), chip]))
                    post(0, m, parts)

    def scatter_second(left):
        for c in range(zc // stride):
            with section("project1_%d" % c):
                ready = []
                for m in range(c * stride, (c + 1) * stride):
                    right = jnp.concatenate(
                        [tile_group(u_tiles, m, core, True), far_group(m, True)], axis=0
                    )
                    ready.append([
                        masked(part, ranks_ref[chip, chip_at(m, h, core, True)])
                        for h, part in enumerate(project(left, right))
                    ])
                for i, parts in enumerate(ready):
                    post(1, c * stride + i, parts)

    def stacked(coeffs):
        wide = coeffs.astype(F32)
        return jnp.concatenate([wide * sign, swap_halves(wide)], axis=0).astype(BF16)

    def expand(left, right):
        return lax.dot_general(
            left, right, (((1,), (1,)), ((), ())), preferred_element_type=F32
        )

    def gathered(block):
        return jnp.concatenate([stacked(part) for part in block], axis=1)

    def collect_first():
        for c in range(steps):
            with section("chipwait0_%d" % c):
                chips_arrived(0, c)
                if c == 0:
                    arrived(u_far, far_recv.at[0])
            with section("expand0_%d" % c):
                members = range(edges[c], edges[c + 1])
                lefts = [gathered([chip_in[0, m * group + h] for h in range(group)]) for m in members]
                for half in (1, 0):
                    total = None if c == 0 and half else image_out[half]
                    for m, left in zip(members, lefts):
                        right = far_group(m, False) if half else tile_group(u_tiles, m, core, False)
                        term = expand(left, right)
                        total = term if total is None else total + term
                    image_out[half] = total
                    if c == steps - 1:
                        image_copy(half).start()
        with section("imagewait"):
            for half in (0, 1):
                image_copy(1 - half).wait_recv()
        return jnp.concatenate([image_out[half] + image_in[half] for half in (0, 1)], axis=1)

    def collect_second():
        def terms(source, c, owner):
            total = None
            for m in range(edges[c], edges[c + 1]):
                left = gathered([source[m * group + h] for h in range(group)])
                term = expand(left, tile_group(v_tiles, m, owner, False))
                total = term if total is None else total + term
            return total

        for c in range(steps + 1):
            if c < steps:
                with section("chipwait1_%d" % c):
                    chips_arrived(1, c)
                share_copy(c).start()
                with section("expand1_%d" % c):
                    term = terms(chip_in.at[1], c, core)
                    total_ref[...] = term if c == 0 else total_ref[...] + term
            if c > 0:
                with section("sharewait1_%d" % (c - 1)):
                    share_copy(c - 1).wait_recv()
                with section("shared1_%d" % (c - 1)):
                    term = total_ref[...] + terms(share_in, c - 1, other)
                    if c < steps:
                        total_ref[...] = term
        return term

    wires = ((band_out, band_in), (thin_out_buf, thin_in), (start_out, start_in))

    def band_copy(p, k):
        target = lax.rem(band + k, bands)
        src, dst = wires[p]
        return pltpu.make_async_remote_copy(
            src_ref=src.at[target], dst_ref=dst.at[band],
            send_sem=sent.at[3 + p], recv_sem=band_recv.at[p],
            device_id={"freq": target}, device_id_type=MESH,
        )

    band_order = [k for k in far_first(bands) if k > 0]

    def to_slabs(values, target):
        for q in range(bands):
            low = q * per_band
            slab = jnp.concatenate(
                [values[low : low + per_band], values[sources + low : sources + low + per_band]],
                axis=0,
            )
            target[q] = slab.astype(target.dtype)

    with section("start"):
        start_load.wait()
        start_t[...] = jnp.transpose(start_rows[...])
        to_slabs(start_t[...], start_out)
        start_in[band] = start_out[band]
    with section("retile_v"):
        retile(v_raw, v_tiles, v_loads)
    scatter_first(
        start_t[...].astype(BF16),
        lambda: pl.semaphore_wait(barrier, zc * group + bands - 1 + core),
    )
    with section("retile_u"):
        retile(u_raw, u_tiles, [u_load])
        for m in range(zc):
            for h in range(group):
                far_copy(m, h).start()
        for k in band_order:
            band_copy(2, k).start()
        observed_load.wait()
        image_out[0] = -jnp.transpose(observed_rows[...])
    misfit = collect_first()
    scatter_second(misfit.astype(BF16))
    change = -STEP_SIZE * collect_second()

    to_slabs(change, band_out)
    for k in band_order:
        band_copy(0, k).start()
    band_in[band] = band_out[band]
    with section("bandwait0"):
        arrived(start_in.at[pl.ds(0, bands - 1)], band_recv.at[2])
        arrived(band_in.at[pl.ds(0, bands - 1)], band_recv.at[0])

    scale = 1.0 / math.sqrt(bands)
    slabs = [start_in[f] + band_in[f].astype(F32) for f in range(bands)]
    reals = [slab[:per_band] for slab in slabs]
    imags = [slab[per_band:] for slab in slabs]
    reals, imags = small_dft(reals, imags, 1.0)
    reals = [thin_out(value * scale) for value in reals]
    imags = [thin_out(value * scale) for value in imags]
    reals, imags = small_dft(reals, imags, -1.0)
    for f in range(bands):
        slab = jnp.concatenate([reals[f], imags[f]], axis=0) * scale
        thin_out_buf[f] = slab.astype(thin_out_buf.dtype)
    for k in band_order:
        band_copy(1, k).start()
    thin_in[band] = thin_out_buf[band]
    with section("bandwait1"):
        arrived(thin_in.at[pl.ds(0, bands - 1)], band_recv.at[1])
    with section("out"):
        slabs = [thin_in[q].astype(F32) for q in range(bands)]
        whole = jnp.concatenate(
            [slab[:per_band] for slab in slabs] + [slab[per_band:] for slab in slabs], axis=0
        )
        out_ref[...] = jnp.transpose(whole)

    with section("tail"):
        departed(pair_out, sent.at[0])
        departed(chip_in.at[1], sent.at[2])
        departed(u_far, sent.at[6])
        departed(image_out, sent.at[7])
        for p in range(3):
            departed(wires[p][0].at[pl.ds(0, bands - 1)], sent.at[3 + p])

        @pl.when(core == 0)
        def _():
            departed(chip_out.at[pl.ds(0, 2 * blocks - 2)], sent.at[1])

        @pl.when(core == 1)
        def _():
            departed(chip_out, sent.at[1])


def body(u_factors, v_factors, ranks, observed, start):
    zc, xc = PLANE
    bands = BANDS
    _, rows, tiles, lanes = u_factors.shape
    width = start.shape[2]
    group = xc // 2
    sources = width // 2
    per_band = sources // bands
    any_spec = pl.BlockSpec(memory_space=pl.ANY)
    block = (zc * group, sources, lanes)
    band_block = (bands, 2 * per_band, rows)
    result = pl.pallas_call(
        kernel,
        out_shape=pltpu.MemorySpace.VMEM((rows, width), F32),
        in_specs=[any_spec] * 5,
        out_specs=pl.BlockSpec(memory_space=pltpu.VMEM),
        scratch_shapes=[
            pltpu.SMEM(ranks.shape[1:], jnp.int32),
            pltpu.VMEM((rows, tiles, lanes), BF16),
            pltpu.VMEM((rows, tiles, lanes), BF16),
            pltpu.VMEM((tiles, rows, lanes), BF16),
            pltpu.VMEM((tiles, rows, lanes), BF16),
            pltpu.VMEM((rows, width), F32),
            pltpu.VMEM((rows, width), F32),
            pltpu.VMEM((width, rows), F32),
            pltpu.VMEM((width, rows), F32),
            pltpu.VMEM((tiles // 2, rows, lanes), BF16),
            pltpu.VMEM((2, width, rows), F32),
            pltpu.VMEM((2, width, rows), F32),
            pltpu.VMEM(block, BF16),
            pltpu.VMEM(block, BF16),
            pltpu.VMEM(block, BF16),
            pltpu.VMEM((2 * zc * group, sources, lanes), BF16),
            pltpu.VMEM((2,) + block, BF16),
            pltpu.VMEM(block, BF16),
            pltpu.VMEM(band_block, F32),
            pltpu.VMEM(band_block, F32),
            pltpu.VMEM(band_block, WIRE_FORTH),
            pltpu.VMEM(band_block, WIRE_FORTH),
            pltpu.VMEM(band_block, WIRE_BACK),
            pltpu.VMEM(band_block, WIRE_BACK),
            pltpu.SemaphoreType.DMA((LOADS + 4,)),
            pltpu.SemaphoreType.DMA((8,)),
            pltpu.SemaphoreType.DMA((max(zc // SPAN, 1),)),
            pltpu.SemaphoreType.DMA((2, len(EDGES))),
            pltpu.SemaphoreType.DMA((len(EDGES),)),
            pltpu.SemaphoreType.DMA((3,)),
            pltpu.SemaphoreType.DMA((1,)),
            pltpu.SemaphoreType.DMA((2,)),
        ],
        compiler_params=pltpu.CompilerParams(collective_id=0, has_side_effects=True),
        name="tile_low_rank_step",
    )(ranks[0], u_factors[0], v_factors[0], observed[0], start[0])
    return result[None]


def solution(mesh):
    in_specs = (
        P("freq", "tile", None, None),
        P("freq", "tile", None, None),
        P("freq", None, None),
        P("freq", "tile", None),
        P("freq", "tile", None),
    )
    out_specs = P("freq", "tile", None)
    return jax.shard_map(body, mesh=mesh, in_specs=in_specs, out_specs=out_specs, check_vma=False)
```

```python
import contextlib
import math

import jax
import jax.numpy as jnp
from jax import lax
from jax.experimental import pallas as pl
from jax.experimental.pallas import tpu as pltpu
from jax.sharding import PartitionSpec as P

STEP_SIZE = 0.2
LEVEL = 0.5
PLANE = (8, 4)
BANDS = 8
MESH = pl.DeviceIdType.MESH
BF16 = jnp.bfloat16
F32 = jnp.float32
SPAN = 4
STRIDE = 4
EDGES = (0, 4, 8)
LOADS = 4
WIRE_FORTH = BF16
WIRE_BACK = BF16


def section(name):
    return contextlib.nullcontext()


def far_first(extent):
    order = sorted(range(extent), key=lambda d: (-min(d, extent - d), d))
    return order


def twiddle_pair(real, imag, cosine, sine):
    if abs(sine) < 1e-9:
        return (real, imag) if cosine > 0 else (-real, -imag)
    if abs(cosine) < 1e-9:
        return (-imag, real) if sine > 0 else (imag, -real)
    return real * cosine - imag * sine, real * sine + imag * cosine


def small_dft(reals, imags, sign):
    count = len(reals)
    if count == 1:
        return reals, imags
    even_re, even_im = small_dft(reals[0::2], imags[0::2], sign)
    odd_re, odd_im = small_dft(reals[1::2], imags[1::2], sign)
    out_re, out_im = [None] * count, [None] * count
    half = count // 2
    for k in range(half):
        angle = sign * 2.0 * math.pi * k / count
        tr, ti = twiddle_pair(odd_re[k], odd_im[k], math.cos(angle), math.sin(angle))
        out_re[k], out_im[k] = even_re[k] + tr, even_im[k] + ti
        out_re[k + half], out_im[k + half] = even_re[k] - tr, even_im[k] - ti
    return out_re, out_im


def thin_out(values):
    return values - jnp.clip(values, -LEVEL, LEVEL)


def kernel(
    ranks_hbm, u_hbm, v_hbm, observed_hbm, start_hbm, out_ref,
    ranks_ref, u_raw, v_raw, u_tiles, v_tiles, observed_rows, start_rows, start_t, total_ref,
    u_far, image_out, image_in,
    pair_out, pair_own, pair_in, chip_out, chip_in, share_in,
    start_out, start_in, band_out, band_in, thin_out_buf, thin_in,
    load_sem, sent, pair_recv, chip_recv, share_recv, band_recv, far_recv, image_recv,
):
    zc, xc = PLANE
    group = xc // 2
    bands = BANDS
    rows = u_raw.shape[0]
    lanes = u_raw.shape[2]
    rank_half = lanes // 2
    sources2 = start_t.shape[0]
    sources = sources2 // 2
    per_band = sources // bands

    place = lax.axis_index("tile")
    band = lax.axis_index("freq")
    chip = lax.div(place, 2)
    core = lax.rem(place, 2)
    other = 1 - core
    z = lax.div(chip, xc)
    x = lax.rem(chip, xc)
    order = far_first(zc)
    span, stride = min(SPAN, zc), min(STRIDE, zc)
    edges = sorted({min(edge, zc) for edge in EDGES})
    steps = len(edges) - 1
    batch_of = [c for c in range(steps) for _ in range(edges[c], edges[c + 1])]
    blocks = zc * group
    self_block = order.index(0) * group

    def shift_of(m, h, owner):
        return 2 * h + lax.rem(owner + order[m], 2)

    def chip_at(m, h, owner, forward):
        dz, dx = order[m], shift_of(m, h, owner)
        if forward:
            return lax.rem(z + dz, zc) * xc + lax.rem(x + dx, xc)
        return lax.rem(z + zc - dz, zc) * xc + lax.rem(x + xc - dx, xc)

    def is_self(m, h):
        return order[m] == 0 and h == 0

    def at_tile(index):
        return {"tile": index}

    barrier = pltpu.get_barrier_semaphore()

    def hail(device):
        pl.semaphore_signal(barrier, inc=1, device_id=device, device_id_type=MESH)

    def hail_all():
        for m in range(zc):
            for h in range(group):
                target = chip_at(m, h, core, True) * 2 + core
                if is_self(m, h):
                    pl.when(core == 1)(lambda target=target: hail(at_tile(target)))
                else:
                    hail(at_tile(target))
        hail(at_tile(chip * 2 + other))
        for k in range(1, bands):
            hail({"freq": lax.rem(band + k, bands)})

    chunk = rows // LOADS

    def chunk_load(source, target, c):
        part = pl.ds(c * chunk, chunk)
        return pltpu.make_async_copy(source.at[part], target.at[part], load_sem.at[c])

    v_loads = [chunk_load(v_hbm, v_raw, c) for c in range(LOADS)]
    u_load = pltpu.make_async_copy(u_hbm, u_raw, load_sem.at[LOADS])
    start_load = pltpu.make_async_copy(start_hbm, start_rows, load_sem.at[LOADS + 1])
    observed_load = pltpu.make_async_copy(observed_hbm, observed_rows, load_sem.at[LOADS + 2])
    hail_all()
    ranks_load = pltpu.make_async_copy(ranks_hbm, ranks_ref, load_sem.at[LOADS + 3])
    start_load.start()
    for load in v_loads:
        load.start()
    ranks_load.start()
    u_load.start()
    observed_load.start()

    def retile(raw, tiles, arrivals):
        def step(b, carry):
            at = pl.multiple_of(b * 16, 16)
            tiles[:, pl.ds(at, 16), :] = jnp.swapaxes(raw[pl.ds(at, 16)], 0, 1)
            return carry

        piece = rows // 16 // len(arrivals)
        for c, load in enumerate(arrivals):
            load.wait()
            lax.fori_loop(c * piece, (c + 1) * piece, step, 0)

    lane_ids = lax.broadcasted_iota(jnp.int32, (sources, lanes), 1)
    upper = lane_ids < rank_half
    rank_ids = jnp.where(upper, lane_ids, lane_ids - rank_half)
    sign = jnp.where(upper, 1.0, -1.0).astype(F32)

    def swap_halves(values):
        return jnp.concatenate([values[:, rank_half:], values[:, :rank_half]], axis=1)

    def tile_group(tiles, m, owner, forward):
        return jnp.concatenate(
            [tiles[chip_at(m, h, owner, forward)] for h in range(group)], axis=1
        )

    def far_group(m, forward):
        return jnp.concatenate(
            [u_far[lax.div(chip_at(m, h, core, forward), 2)] for h in range(group)], axis=1
        )

    def pair_copy(c):
        part = pl.ds(c * span * group, span * group)
        return pltpu.make_async_remote_copy(
            src_ref=pair_out.at[part], dst_ref=pair_in.at[part],
            send_sem=sent.at[0], recv_sem=pair_recv.at[c],
            device_id=at_tile(chip * 2 + other), device_id_type=MESH,
        )

    def chip_copy(p, m, h):
        block = m * group + h
        return pltpu.make_async_remote_copy(
            src_ref=chip_out.at[p * blocks + block], dst_ref=chip_in.at[p, block],
            send_sem=sent.at[1], recv_sem=chip_recv.at[p, batch_of[m]],
            device_id=at_tile(chip_at(m, h, core, True) * 2 + core), device_id_type=MESH,
        )

    def share_copy(c):
        part = pl.ds(edges[c] * group, (edges[c + 1] - edges[c]) * group)
        return pltpu.make_async_remote_copy(
            src_ref=chip_in.at[1, part], dst_ref=share_in.at[part],
            send_sem=sent.at[2], recv_sem=share_recv.at[c],
            device_id=at_tile(chip * 2 + other), device_id_type=MESH,
        )

    def far_copy(m, h):
        tile = chip_at(m, h, other, True)
        return pltpu.make_async_remote_copy(
            src_ref=u_tiles.at[tile], dst_ref=u_far.at[lax.div(tile, 2)],
            send_sem=sent.at[6], recv_sem=far_recv.at[0],
            device_id=at_tile(chip * 2 + other), device_id_type=MESH,
        )

    def image_copy(half):
        return pltpu.make_async_remote_copy(
            src_ref=image_out.at[half], dst_ref=image_in.at[1 - half],
            send_sem=sent.at[7], recv_sem=image_recv.at[1 - half],
            device_id=at_tile(chip * 2 + other), device_id_type=MESH,
        )

    def arrived(target, sem):
        pltpu.make_async_remote_copy(
            src_ref=target, dst_ref=target, send_sem=sent.at[0], recv_sem=sem,
            device_id=at_tile(chip * 2 + other), device_id_type=MESH,
        ).wait_recv()

    def departed(source, sem):
        pltpu.make_async_remote_copy(
            src_ref=source, dst_ref=source, send_sem=sem, recv_sem=band_recv.at[0],
            device_id=at_tile(chip * 2 + other), device_id_type=MESH,
        ).wait_send()

    def chips_arrived(p, c):
        first, count = edges[c] * group, (edges[c + 1] - edges[c]) * group
        sem = chip_recv.at[p, c]
        if first <= self_block < first + count:
            @pl.when(core == 0)
            def _():
                if count > 1:
                    arrived(chip_in.at[p, pl.ds(first, count - 1)], sem)

            @pl.when(core == 1)
            def _():
                arrived(chip_in.at[p, pl.ds(first, count)], sem)
        else:
            arrived(chip_in.at[p, pl.ds(first, count)], sem)

    def remote_only(m, h, act):
        if is_self(m, h):
            pl.when(core == 1)(act)
        else:
            act()

    def project(left, right):
        product = jnp.dot(left, right, preferred_element_type=F32)
        parts = []
        for h in range(group):
            block = product[:, h * lanes : (h + 1) * lanes]
            parts.append(block[:sources] * sign + swap_halves(block[sources:]))
        return parts

    def masked(part, rank):
        return jnp.where(rank_ids < rank, part, 0.0).astype(BF16)

    def post(p, m, parts):
        for h, part in enumerate(parts):
            block = m * group + h
            chip_out[p * blocks + block] = part
            if is_self(m, h):
                @pl.when(core == 0)
                def _(part=part, block=block):
                    chip_in[p, block] = part

        for h in (reversed(range(group)) if p == 0 else range(group)):
            remote_only(m, h, lambda m=m, h=h: chip_copy(p, m, h).start())

    chunks = range(zc // span)

    def scatter_first(left, ready):
        def fill(target, owner):
            for m in range(zc):
                for h, part in enumerate(project(left, tile_group(v_tiles, m, owner, True))):
                    target[m * group + h] = part.astype(BF16)

        with section("give0"):
            fill(pair_out, other)
        with section("keep0"):
            fill(pair_own, core)
            ranks_load.wait()
        with section("ready"):
            ready()
        for c in chunks:
            pair_copy(c).start()
        for c in chunks:
            with section("pairwait0_%d" % c):
                pair_copy(c).wait_recv()
            with section("finish0_%d" % c):
                for m in range(c * span, (c + 1) * span):
                    parts = []
                    for h in range(group):
                        block = m * group + h
                        total = pair_own[block].astype(F32) + pair_in[block].astype(F32)
                        parts.append(masked(total, ranks_ref[chip_at(m, h, core, True), chip]))
                    post(0, m, parts)

    def scatter_second(left):
        for c in range(zc // stride):
            with section("project1_%d" % c):
                ready = []
                for m in range(c * stride, (c + 1) * stride):
                    right = jnp.concatenate(
                        [tile_group(u_tiles, m, core, True), far_group(m, True)], axis=0
                    )
                    ready.append([
                        masked(part, ranks_ref[chip, chip_at(m, h, core, True)])
                        for h, part in enumerate(project(left, right))
                    ])
                for i, parts in enumerate(ready):
                    post(1, c * stride + i, parts)

    def stacked(coeffs):
        wide = coeffs.astype(F32)
        return jnp.concatenate([wide * sign, swap_halves(wide)], axis=0).astype(BF16)

    def expand(left, right):
        return lax.dot_general(
            left, right, (((1,), (1,)), ((), ())), preferred_element_type=F32
        )

    def gathered(block):
        return jnp.concatenate([stacked(part) for part in block], axis=1)

    def collect_first():
        for c in range(steps):
            with section("chipwait0_%d" % c):
                chips_arrived(0, c)
                if c == 0:
                    arrived(u_far, far_recv.at[0])
            with section("expand0_%d" % c):
                members = range(edges[c], edges[c + 1])
                lefts = [gathered([chip_in[0, m * group + h] for h in range(group)]) for m in members]
                for half in (1, 0):
                    total = None if c == 0 and half else image_out[half]
                    for m, left in zip(members, lefts):
                        right = far_group(m, False) if half else tile_group(u_tiles, m, core, False)
                        term = expand(left, right)
                        total = term if total is None else total + term
                    image_out[half] = total
                    if c == steps - 1:
                        image_copy(half).start()
        with section("imagewait"):
            for half in (0, 1):
                image_copy(1 - half).wait_recv()
        return jnp.concatenate([image_out[half] + image_in[half] for half in (0, 1)], axis=1)

    def collect_second():
        def terms(source, c, owner):
            total = None
            for m in range(edges[c], edges[c + 1]):
                left = gathered([source[m * group + h] for h in range(group)])
                term = expand(left, tile_group(v_tiles, m, owner, False))
                total = term if total is None else total + term
            return total

        for c in range(steps + 1):
            if c < steps:
                with section("chipwait1_%d" % c):
                    chips_arrived(1, c)
                share_copy(c).start()
                with section("expand1_%d" % c):
                    term = terms(chip_in.at[1], c, core)
                    total_ref[...] = term if c == 0 else total_ref[...] + term
            if c > 0:
                with section("sharewait1_%d" % (c - 1)):
                    share_copy(c - 1).wait_recv()
                with section("shared1_%d" % (c - 1)):
                    term = total_ref[...] + terms(share_in, c - 1, other)
                    if c < steps:
                        total_ref[...] = term
        return term

    wires = ((band_out, band_in), (thin_out_buf, thin_in), (start_out, start_in))

    def band_copy(p, k):
        target = lax.rem(band + k, bands)
        src, dst = wires[p]
        return pltpu.make_async_remote_copy(
            src_ref=src.at[target], dst_ref=dst.at[band],
            send_sem=sent.at[3 + p], recv_sem=band_recv.at[p],
            device_id={"freq": target}, device_id_type=MESH,
        )

    band_order = [k for k in far_first(bands) if k > 0]

    def to_slabs(values, target):
        for q in range(bands):
            low = q * per_band
            slab = jnp.concatenate(
                [values[low : low + per_band], values[sources + low : sources + low + per_band]],
                axis=0,
            )
            target[q] = slab.astype(target.dtype)

    with section("start"):
        start_load.wait()
        start_t[...] = jnp.transpose(start_rows[...])
        to_slabs(start_t[...], start_out)
        start_in[band] = start_out[band]
    with section("retile_v"):
        retile(v_raw, v_tiles, v_loads)
    scatter_first(
        start_t[...].astype(BF16),
        lambda: pl.semaphore_wait(barrier, zc * group + bands - 1 + core),
    )
    with section("retile_u"):
        retile(u_raw, u_tiles, [u_load])
        for m in range(zc):
            for h in range(group):
                far_copy(m, h).start()
        for k in band_order:
            band_copy(2, k).start()
        observed_load.wait()
        image_out[0] = -jnp.transpose(observed_rows[...])
    misfit = collect_first()
    scatter_second(misfit.astype(BF16))
    change = -STEP_SIZE * collect_second()

    to_slabs(change, band_out)
    for k in band_order:
        band_copy(0, k).start()
    band_in[band] = band_out[band]
    with section("bandwait0"):
        arrived(start_in.at[pl.ds(0, bands - 1)], band_recv.at[2])
        arrived(band_in.at[pl.ds(0, bands - 1)], band_recv.at[0])

    scale = 1.0 / math.sqrt(bands)
    slabs = [start_in[f] + band_in[f].astype(F32) for f in range(bands)]
    reals = [slab[:per_band] for slab in slabs]
    imags = [slab[per_band:] for slab in slabs]
    reals, imags = small_dft(reals, imags, 1.0)
    reals = [thin_out(value * scale) for value in reals]
    imags = [thin_out(value * scale) for value in imags]
    reals, imags = small_dft(reals, imags, -1.0)
    for f in range(bands):
        slab = jnp.concatenate([reals[f], imags[f]], axis=0) * scale
        thin_out_buf[f] = slab.astype(thin_out_buf.dtype)
    for k in band_order:
        band_copy(1, k).start()
    thin_in[band] = thin_out_buf[band]
    with section("bandwait1"):
        arrived(thin_in.at[pl.ds(0, bands - 1)], band_recv.at[1])
    with section("out"):
        slabs = [thin_in[q].astype(F32) for q in range(bands)]
        whole = jnp.concatenate(
            [slab[:per_band] for slab in slabs] + [slab[per_band:] for slab in slabs], axis=0
        )
        out_ref[...] = jnp.transpose(whole)

    with section("tail"):
        departed(pair_out, sent.at[0])
        departed(chip_in.at[1], sent.at[2])
        departed(u_far, sent.at[6])
        departed(image_out, sent.at[7])
        for p in range(3):
            departed(wires[p][0].at[pl.ds(0, bands - 1)], sent.at[3 + p])

        @pl.when(core == 0)
        def _():
            departed(chip_out.at[pl.ds(0, 2 * blocks - 2)], sent.at[1])

        @pl.when(core == 1)
        def _():
            departed(chip_out, sent.at[1])


def body(u_factors, v_factors, ranks, observed, start):
    zc, xc = PLANE
    bands = BANDS
    _, rows, tiles, lanes = u_factors.shape
    width = start.shape[2]
    group = xc // 2
    sources = width // 2
    per_band = sources // bands
    any_spec = pl.BlockSpec(memory_space=pl.ANY)
    block = (zc * group, sources, lanes)
    band_block = (bands, 2 * per_band, rows)
    result = pl.pallas_call(
        kernel,
        out_shape=pltpu.MemorySpace.VMEM((rows, width), F32),
        in_specs=[any_spec] * 5,
        out_specs=pl.BlockSpec(memory_space=pltpu.VMEM),
        scratch_shapes=[
            pltpu.SMEM(ranks.shape[1:], jnp.int32),
            pltpu.VMEM((rows, tiles, lanes), BF16),
            pltpu.VMEM((rows, tiles, lanes), BF16),
            pltpu.VMEM((tiles, rows, lanes), BF16),
            pltpu.VMEM((tiles, rows, lanes), BF16),
            pltpu.VMEM((rows, width), F32),
            pltpu.VMEM((rows, width), F32),
            pltpu.VMEM((width, rows), F32),
            pltpu.VMEM((width, rows), F32),
            pltpu.VMEM((tiles // 2, rows, lanes), BF16),
            pltpu.VMEM((2, width, rows), F32),
            pltpu.VMEM((2, width, rows), F32),
            pltpu.VMEM(block, BF16),
            pltpu.VMEM(block, BF16),
            pltpu.VMEM(block, BF16),
            pltpu.VMEM((2 * zc * group, sources, lanes), BF16),
            pltpu.VMEM((2,) + block, BF16),
            pltpu.VMEM(block, BF16),
            pltpu.VMEM(band_block, F32),
            pltpu.VMEM(band_block, F32),
            pltpu.VMEM(band_block, WIRE_FORTH),
            pltpu.VMEM(band_block, WIRE_FORTH),
            pltpu.VMEM(band_block, WIRE_BACK),
            pltpu.VMEM(band_block, WIRE_BACK),
            pltpu.SemaphoreType.DMA((LOADS + 4,)),
            pltpu.SemaphoreType.DMA((8,)),
            pltpu.SemaphoreType.DMA((max(zc // SPAN, 1),)),
            pltpu.SemaphoreType.DMA((2, len(EDGES))),
            pltpu.SemaphoreType.DMA((len(EDGES),)),
            pltpu.SemaphoreType.DMA((3,)),
            pltpu.SemaphoreType.DMA((1,)),
            pltpu.SemaphoreType.DMA((2,)),
        ],
        compiler_params=pltpu.CompilerParams(collective_id=0, has_side_effects=True),
        name="tile_low_rank_step",
    )(ranks[0], u_factors[0], v_factors[0], observed[0], start[0])
    return result[None]


def solution(mesh):
    in_specs = (
        P("freq", "tile", None, None),
        P("freq", "tile", None, None),
        P("freq", None, None),
        P("freq", "tile", None),
        P("freq", "tile", None),
    )
    out_specs = P("freq", "tile", None)
    return jax.shard_map(body, mesh=mesh, in_specs=in_specs, out_specs=out_specs, check_vma=False)
```
